32 devices in a mesh: dp: 8 (over y, x, core), fsdp: 4 (over z).
Axes of the slice: x: 2, y: 2, z: 4, core: 2. Of those that a mesh axis runs over, the one named last changes fastest.
Arguments:
- hidden_in: bfloat16 [16384, 768], P(('dp', 'fsdp')), may hold values from -32 to 32
- norm_gain: float32 [768], replicated, may hold values from 0.1 to 1.9
- qkv_weight: bfloat16 [768, 2304], P('fsdp'), may hold values from -9.237604 to 9.237604
- out_weight: bfloat16 [768, 768], P('fsdp'), may hold values from -0.21875 to 0.21875
- final_gain: float32 [768], replicated, may hold values from 0.1 to 1.9
- head_weight: bfloat16 [768, 128], P('fsdp'), may hold values from -0.21875 to 0.21875
- queries: bfloat16 [64, 32, 128], P(('dp', 'fsdp')), may hold values from -6 to 6
- query_lengths: int32 [64], P(('dp', 'fsdp')), may hold values from 8 to 32, as said below
- passage_lengths: int32 [64], P(('dp', 'fsdp')), may hold values from 64 to 256, as said below
- partner: int32 [8], replicated, may hold values from 0 to 7, as said below
Outputs:
- losses: float32 [64], P(('dp', 'fsdp'))
- grad_input: bfloat16 [16384, 768], P(('dp', 'fsdp'))
- grad_out_proj: float32 [768, 768], P('fsdp')
- grad_head: float32 [768, 128], P('fsdp')
The draws below stay inside these ranges and needn't reach their ends.
Inputs may be any that keep to these rules, and one draw needn't show every extreme that they name: `passage_lengths`: some passage has all 256 slots live. `query_lengths`: some query has all 32 slots live. A permutation of the 8 dp indices with partner[r] != r for every r.
All inputs are finite; a program needn't handle non-finite values.
Results may differ from the reference program's by a relative error of at most 0.02.
The reference program's roundings to bfloat16 on the way count: a program that leaves them out, or rounds other values in their place, can miss the bound.
Values may be sent and summed in bfloat16 or wider, within the bound.
A program may use at most 64 MiB of HBM per device.

```python
import math
import jax
import jax.numpy as jnp
from jax import lax

D = 768
HEADS = 12
CDIM = 128
WIN = 64
PLEN = 256
QLEN = 32
PASS_DEV = 2
PASSAGES = 64
QUERIES = 64
TOKENS = 16384
PEERS = 8
N_DP = 8
N_FSDP = 4


def draw_hidden_in(key, part):
    base_key = jax.random.fold_in(key, 101)
    key_main, key_rows, key_cols = jax.random.split(base_key, 3)
    main_part = jax.random.truncated_normal(key_main, -4.0, 4.0, (TOKENS, D), jnp.float32)
    row_scale = jnp.exp(jax.random.uniform(key_rows, (TOKENS, 1), jnp.float32, math.log(0.3), math.log(3.0)))
    col_scale = jnp.exp(jax.random.uniform(key_cols, (1, D), jnp.float32, math.log(0.5), math.log(2.0)))
    return (main_part * row_scale * col_scale).astype(jnp.bfloat16)


def draw_qkv_weight(key, part):
    base_key = jax.random.fold_in(key, 202)
    key_main = jax.random.fold_in(base_key, 0)
    base = jax.random.truncated_normal(key_main, -4.0, 4.0, (D, 3 * D), jnp.float32) * D ** (-0.5)
    return base.astype(jnp.bfloat16)


def draw_passage_lengths(key, part):
    base_key = jax.random.fold_in(key, 303)
    key_len, key_full = jax.random.split(base_key, 2)
    lengths = jax.random.randint(key_len, (PASSAGES,), PLEN // 4, PLEN + 1, jnp.int32)
    chosen = jax.random.randint(key_full, (), 0, PASSAGES, jnp.int32)
    return lengths.at[chosen].set(PLEN)


def draw_query_lengths(key, part):
    base_key = jax.random.fold_in(key, 404)
    key_len, key_full = jax.random.split(base_key, 2)
    lengths = jax.random.randint(key_len, (QUERIES,), QLEN // 4, QLEN + 1, jnp.int32)
    chosen = jax.random.randint(key_full, (), 0, QUERIES, jnp.int32)
    return lengths.at[chosen].set(QLEN)


def draw_partner(key, part):
    base_key = jax.random.fold_in(key, 505)
    order = jax.random.permutation(base_key, PEERS).astype(jnp.int32)
    return jnp.zeros((PEERS,), jnp.int32).at[order].set(jnp.roll(order, -1))


def block_scale(own_key, dims, cuts, smallest, top_value):
    factor_of = 1.0
    for axis_at, blocks in cuts:
        draws = jax.random.uniform(jax.random.fold_in(jax.random.fold_in(own_key, 6), axis_at), (blocks,), jnp.float32, smallest / len(cuts), top_value / len(cuts))
        factor_of = factor_of * jnp.repeat(jnp.exp(draws), dims[axis_at] // blocks).reshape((-1,) + (1,) * (len(dims) - 1 - axis_at))
    return factor_of


def noise(key, shape, deviation, reach, cuts=(), kind=jnp.bfloat16):
    result = jax.random.normal(key, shape, jnp.float32) * deviation
    if len(cuts) > 0:
        result = block_scale(key, shape, cuts, -0.22, 0.18) * result
    return jnp.clip(result, min=-reach, max=reach).astype(kind)


def setup_inputs(seed: int = 0) -> dict:
    seeds = jax.random.split(jax.random.key(seed), 11)
    hidden_in = draw_hidden_in(jax.random.fold_in(seeds[10], 71), 0)
    norm_gain = jnp.clip(1.0 + 0.18 * jax.random.normal(seeds[1], (D,), jnp.float32), 0.1, 1.9)
    qkv_weight = draw_qkv_weight(jax.random.fold_in(seeds[10], 71), 0)
    out_weight = noise(seeds[3], (D, D), D ** -0.5, 0.21875, ((0, 4),))
    final_gain = jnp.clip(1.0 + 0.18 * jax.random.normal(seeds[4], (D,), jnp.float32), 0.1, 1.9)
    head_weight = noise(seeds[5], (D, CDIM), D ** -0.5, 0.21875, ((0, 4),))
    queries = noise(seeds[6], (QUERIES, QLEN, CDIM), 1.0, 6.0, ((0, 32),))
    query_lengths = draw_query_lengths(jax.random.fold_in(seeds[10], 71), 0)
    passage_lengths = draw_passage_lengths(jax.random.fold_in(seeds[10], 71), 0)
    partner = draw_partner(jax.random.fold_in(seeds[10], 71), 0)
    return dict(hidden_in=hidden_in, norm_gain=norm_gain, qkv_weight=qkv_weight, out_weight=out_weight, final_gain=final_gain, head_weight=head_weight, queries=queries, query_lengths=query_lengths, passage_lengths=passage_lengths, partner=partner)


norm_eps = 1e-05
vec_eps = 1e-06
soft_temp = 0.05
masked_fill = -1e+30

def layer_stats(rows):
    centered = rows - lax.optimization_barrier(jnp.mean(rows, axis=-1, keepdims=True))
    inv_std = lax.rsqrt(lax.optimization_barrier(jnp.mean(centered * centered, axis=-1, keepdims=True)) + norm_eps)
    return (centered * inv_std, inv_std)

def layer_back(grad_out, gain, normed, inv_std):
    scaled = grad_out * gain
    return inv_std * (scaled - lax.optimization_barrier(jnp.mean(scaled, axis=-1, keepdims=True)) - normed * lax.optimization_barrier(jnp.mean(scaled * normed, axis=-1, keepdims=True)))

def band_allowed(live_mask):
    position = jnp.arange(PLEN)
    in_band = jnp.abs(position[:, None] - position[None, :]) <= WIN
    is_self = position[:, None] == position[None, :]
    return in_band[None] & ((live_mask[:, None, :] > 0.5) | is_self[None])

def split_heads(matrix):
    count = matrix.shape[0] // PLEN
    return matrix.reshape(count, PLEN, HEADS, D // HEADS).transpose(2, 0, 1, 3)

def merge_heads(stacked):
    count = stacked.shape[1]
    return stacked.transpose(1, 2, 0, 3).reshape(count * PLEN, D)

def head_probs(q_head, k_head, allowed):
    scores = jnp.einsum('pid,pjd->pij', q_head.astype(jnp.float32), k_head.astype(jnp.float32))
    scores = jnp.where(allowed, scores, masked_fill)
    shifted = jnp.exp(scores - lax.optimization_barrier(jnp.max(scores, axis=-1, keepdims=True)))
    return shifted / lax.optimization_barrier(jnp.sum(shifted, axis=-1, keepdims=True))

def encode(hidden_rows, norm_gain, qkv_weight, out_weight, final_gain, head_weight, live_mask):
    head_scale = (D // HEADS) ** (-0.5)
    hidden_f32 = hidden_rows.astype(jnp.float32)
    normed_in, inv_in = layer_stats(hidden_f32)
    normed_b = (normed_in * norm_gain).astype(jnp.bfloat16)
    proj_qkv = jnp.dot(normed_b, qkv_weight, preferred_element_type=jnp.float32)
    q_rows = (proj_qkv[:, :D] * head_scale).astype(jnp.bfloat16)
    k_rows = proj_qkv[:, D:2 * D].astype(jnp.bfloat16)
    v_rows = proj_qkv[:, 2 * D:].astype(jnp.bfloat16)
    allowed = band_allowed(live_mask)

    def one_head(operands):
        q_head, k_head, v_head = operands
        probs_b = head_probs(q_head, k_head, allowed).astype(jnp.bfloat16)
        return jnp.einsum('pij,pjd->pid', probs_b.astype(jnp.float32), v_head.astype(jnp.float32)).astype(jnp.bfloat16)
    context = merge_heads(lax.map(one_head, (split_heads(q_rows), split_heads(k_rows), split_heads(v_rows))))
    residual = hidden_f32 + jnp.dot(context, out_weight, preferred_element_type=jnp.float32)
    normed_res, inv_res = layer_stats(residual)
    pooled = (normed_res * final_gain).astype(jnp.bfloat16)
    embedded = jnp.dot(pooled, head_weight, preferred_element_type=jnp.float32)
    inv_len = lax.rsqrt(lax.optimization_barrier(jnp.sum(embedded * embedded, axis=-1, keepdims=True)) + vec_eps)
    vectors = (embedded * inv_len).astype(jnp.bfloat16)
    return dict(normed_in=normed_in, inv_in=inv_in, q_rows=q_rows, k_rows=k_rows, v_rows=v_rows, allowed=allowed, context=context, normed_res=normed_res, inv_res=inv_res, pooled=pooled, embedded=embedded, inv_len=inv_len, vectors=vectors)

def soft_sims(query_vecs, query_mask, passage_vecs, passage_live):
    similar = jnp.einsum('aic,bjc->aibj', query_vecs.astype(jnp.float32), passage_vecs.astype(jnp.float32))
    sim_weight = jnp.exp(similar / soft_temp) * passage_live[None, None]
    return (sim_weight, lax.optimization_barrier(jnp.sum(sim_weight, axis=-1)))

def sim_scores(query_vecs, query_mask, passage_vecs, passage_live):
    sim_weight, denominator = soft_sims(query_vecs, query_mask, passage_vecs, passage_live)
    return lax.optimization_barrier(jnp.sum(query_mask[:, :, None] * soft_temp * jnp.log(denominator), axis=1))

def sim_back(query_vecs, query_mask, passage_vecs, passage_live, match_grad):
    sim_weight, denominator = soft_sims(query_vecs, query_mask, passage_vecs, passage_live)
    sim_grad = match_grad[:, None, :, None] * query_mask[:, :, None, None] * sim_weight / denominator[..., None]
    sim_grad = sim_grad.astype(jnp.bfloat16)
    return jnp.einsum('aibj,aic->bjc', sim_grad.astype(jnp.float32), query_vecs.astype(jnp.float32))

def contrast(local_match, far_match):
    count = local_match.shape[0]
    logits = jnp.concatenate([local_match, far_match], axis=1)
    log_total = jnp.log(lax.optimization_barrier(jnp.sum(jnp.exp(logits), axis=1)))
    losses = log_total - jnp.diagonal(local_match)
    soft = jnp.exp(logits - log_total[:, None])
    identity = jnp.eye(count, dtype=soft.dtype)
    return (losses, soft[:, :count] - identity, soft[:, count:])

def backward(parts, norm_gain, qkv_weight, out_weight, final_gain, head_weight, vector_grad):
    head_scale = (D // HEADS) ** (-0.5)
    embedded = parts['embedded']
    inv_len = parts['inv_len']
    along = lax.optimization_barrier(jnp.sum(embedded * vector_grad, axis=-1, keepdims=True))
    emb_grad = (inv_len * vector_grad - embedded * inv_len ** 3 * along).astype(jnp.bfloat16)
    head_term = jnp.dot(parts['pooled'].T, emb_grad, preferred_element_type=jnp.float32)
    pool_grad = jnp.dot(emb_grad, head_weight.T, preferred_element_type=jnp.float32)
    res_grad = layer_back(pool_grad, final_gain, parts['normed_res'], parts['inv_res'])
    res_grad_b = res_grad.astype(jnp.bfloat16)
    out_term = jnp.dot(parts['context'].T, res_grad_b, preferred_element_type=jnp.float32)
    context_grad = jnp.dot(res_grad_b, out_weight.T, preferred_element_type=jnp.float32).astype(jnp.bfloat16)
    allowed = parts['allowed']

    def one_head(operands):
        q_head, k_head, v_head, d_head = operands
        attn_probs = head_probs(q_head, k_head, allowed)
        probs_b = attn_probs.astype(jnp.bfloat16).astype(jnp.float32)
        d_f32 = d_head.astype(jnp.float32)
        prob_grad = jnp.einsum('pid,pjd->pij', d_f32, v_head.astype(jnp.float32))
        val_grad = jnp.einsum('pij,pid->pjd', probs_b, d_f32)
        score_grad = attn_probs * (prob_grad - lax.optimization_barrier(jnp.sum(attn_probs * prob_grad, axis=-1, keepdims=True)))
        score_grad = score_grad.astype(jnp.bfloat16).astype(jnp.float32)
        query_grad = jnp.einsum('pij,pjd->pid', score_grad, k_head.astype(jnp.float32)) * head_scale
        key_grad = jnp.einsum('pij,pid->pjd', score_grad, q_head.astype(jnp.float32))
        return (query_grad, key_grad, val_grad)
    query_grad, key_grad, val_grad = lax.map(one_head, (split_heads(parts['q_rows']), split_heads(parts['k_rows']), split_heads(parts['v_rows']), split_heads(context_grad)))
    qkv_grad = jnp.concatenate([merge_heads(query_grad), merge_heads(key_grad), merge_heads(val_grad)], axis=1).astype(jnp.bfloat16)
    in_grad = jnp.dot(qkv_grad, qkv_weight.T, preferred_element_type=jnp.float32)
    grad_rows = res_grad + layer_back(in_grad, norm_gain, parts['normed_in'], parts['inv_in'])
    return (grad_rows.astype(jnp.bfloat16), out_term, head_term)

def reference(hidden_in, norm_gain, qkv_weight, out_weight, final_gain, head_weight, queries, query_lengths, passage_lengths, partner):
    devices_all = N_DP * N_FSDP
    tok_count = PASS_DEV * PLEN
    hidden_dev = hidden_in.reshape(devices_all, tok_count, D)
    live_all = (jnp.arange(PLEN)[None, None, :] < passage_lengths.reshape(devices_all, PASS_DEV)[:, :, None]).astype(jnp.float32)
    query_f32 = queries.astype(jnp.float32)
    query_vecs = (query_f32 * lax.rsqrt(lax.optimization_barrier(jnp.sum(query_f32 * query_f32, axis=-1, keepdims=True)) + vec_eps)).astype(jnp.bfloat16)
    query_vecs = query_vecs.reshape(devices_all, PASS_DEV, QLEN, CDIM)
    query_mask = (jnp.arange(QLEN)[None, :] < query_lengths[:, None]).astype(jnp.float32).reshape(devices_all, PASS_DEV, QLEN)

    def encode_device(device_item):
        hidden_rows, live_mask = device_item
        parts = encode(hidden_rows, norm_gain, qkv_weight, out_weight, final_gain, head_weight, live_mask)
        return parts['vectors'].reshape(PASS_DEV, PLEN, CDIM)
    vectors = lax.map(encode_device, (hidden_dev, live_all))
    dev_ids = jnp.arange(devices_all, dtype=jnp.int32)
    targets = (partner[dev_ids // N_FSDP] * N_FSDP + dev_ids % N_FSDP).astype(jnp.int32)
    inverse = jnp.zeros((N_DP,), jnp.int32).at[partner].set(jnp.arange(N_DP, dtype=jnp.int32))
    sources = (inverse[dev_ids // N_FSDP] * N_FSDP + dev_ids % N_FSDP).astype(jnp.int32)

    def score_device(index):
        local_match = sim_scores(query_vecs[index], query_mask[index], vectors[index], live_all[index])
        far_vecs = vectors[targets[index]]
        far_live = live_all[targets[index]]
        far_match = sim_scores(query_vecs[index], query_mask[index], far_vecs, far_live)
        losses, local_grad, far_grad_m = contrast(local_match, far_match)
        near_grad = sim_back(query_vecs[index], query_mask[index], vectors[index], live_all[index], local_grad)
        far_grad = sim_back(query_vecs[index], query_mask[index], far_vecs, far_live, far_grad_m).astype(jnp.bfloat16)
        return (losses, near_grad, far_grad)
    losses, near_grad, far_grad = lax.map(score_device, dev_ids)
    far_grad = lax.optimization_barrier(far_grad)
    vector_grad = near_grad + far_grad[sources].astype(jnp.float32)
    vector_grad = vector_grad.reshape(devices_all, tok_count, CDIM)

    def back_device(carry, device_item):
        hidden_rows, live_mask, grad_rows = device_item
        parts = encode(hidden_rows, norm_gain, qkv_weight, out_weight, final_gain, head_weight, live_mask)
        grad_in, out_term, head_term = backward(parts, norm_gain, qkv_weight, out_weight, final_gain, head_weight, grad_rows)
        return ((carry[0] + out_term, carry[1] + head_term), grad_in)
    start_carry = (jnp.zeros((D, D), jnp.float32), jnp.zeros((D, CDIM), jnp.float32))
    sums, grad_input = lax.scan(back_device, start_carry, (hidden_dev, live_all, vector_grad))
    return (losses.reshape(QUERIES), grad_input.reshape(TOKENS, D), sums[0], sums[1])
```

```python
import functools

import jax
import jax.numpy as jnp
from jax import lax
from jax.experimental import pallas as pl
from jax.experimental.pallas import tpu as pltpu
from jax.sharding import PartitionSpec as P

D = 768
HEADS = 12
HD = D // HEADS
CDIM = 128
WIN = 64
PLEN = 256
QLEN = 32
NB = 256
RB = 128

norm_eps = 1e-05
vec_eps = 1e-06
soft_temp = 0.05
masked_fill = -1e30

MESH = pl.DeviceIdType.MESH
F32 = jnp.float32
BF16 = jnp.bfloat16


def dot_nn(a, b):
    return lax.dot_general(a, b, (((1,), (0,)), ((), ())), preferred_element_type=F32)


def dot_nt(a, b):
    return lax.dot_general(a, b, (((1,), (1,)), ((), ())), preferred_element_type=F32)


def dot_tn(a, b):
    return lax.dot_general(a, b, (((0,), (0,)), ((), ())), preferred_element_type=F32)


def stats(rows):
    centered = rows - jnp.mean(rows, axis=-1, keepdims=True)
    inv_std = lax.rsqrt(jnp.mean(centered * centered, axis=-1, keepdims=True) + norm_eps)
    return centered * inv_std, inv_std


def row_loop(count, body):
    def step(i, carry):
        body(pl.ds(pl.multiple_of(i * RB, RB), RB))
        return carry

    lax.fori_loop(0, count // RB, step, 0)


def block_loop(count, body):
    def step(n, carry):
        body(n, pl.ds(pl.multiple_of(n * NB, NB), NB))
        return carry

    lax.fori_loop(0, count // NB, step, 0)


def fill_bias(len_ref, bias, passages):
    row = lax.broadcasted_iota(jnp.int32, (PLEN, PLEN), 0)
    col = lax.broadcasted_iota(jnp.int32, (PLEN, PLEN), 1)
    in_band = jnp.abs(row - col) <= WIN
    for p in range(passages):
        allowed = in_band & ((row < len_ref[p]) | (row == col))
        bias[p] = jnp.where(allowed, 0.0, masked_fill)


def half_masks():
    lane = lax.broadcasted_iota(jnp.int32, (PLEN, 128), 1)
    low = lane < HD
    keep = jnp.where(low, 1.0, 0.0)
    return low, (keep.astype(BF16), (1.0 - keep).astype(BF16))


def probs_of(q_masked, k_pair, bias):
    scores = dot_nt(k_pair, q_masked) + bias
    shifted = jnp.exp(scores - jnp.max(scores, axis=0, keepdims=True))
    return shifted * (1.0 / jnp.sum(shifted, axis=0, keepdims=True))


def greet(peers):
    barrier = pltpu.get_barrier_semaphore()
    for peer in peers:
        pl.semaphore_signal(barrier, inc=1, device_id=peer, device_id_type=MESH)
    return lambda: pl.semaphore_wait(barrier, len(peers))


def send(src, dst, sems, at, peer):
    copy = pltpu.make_async_remote_copy(
        src_ref=src,
        dst_ref=dst,
        send_sem=sems[0].at[at],
        recv_sem=sems[1].at[at],
        device_id=peer,
        device_id_type=MESH,
    )
    copy.start()
    return copy


GROUPS = 3
GW = D // GROUPS


def head_at(g, w):
    return pl.multiple_of(g * 3 * GW + w * 128, 128)


def step_kernel(
    n_dp,
    n_f,
    gathered,
    x_hbm,
    len_ref,
    qlen_ref,
    partner_ref,
    gain_ref,
    fgain_ref,
    quer_ref,
    qkvw_ref,
    outw_hbm,
    headw_hbm,
    gin_ref,
    gout_ref,
    ghead_ref,
    loss_ref,
    x_ref,
    w_ref,
    outw_ref,
    headw_ref,
    qkv_ref,
    ctx_ref,
    pack_ref,
    normed,
    mine,
    res,
    inv_res,
    pooled,
    emb,
    rgb,
    rg_ref,
    dctx_ref,
    wgrad_ref,
    grads,
    bias,
    saved,
    tile,
    got,
    stage,
    r0,
    pre,
    r1,
    acc,
    s2,
    r2,
    s3,
    r3,
    *sems,
):
    q_sems, m_sems, g0_sems, g1_sems, g2_sems, g3_sems = [
        sems[2 * i : 2 * i + 2] for i in range(6)
    ]
    l_sem = sems[12]
    rows_all = x_ref.shape[0]
    passages = rows_all // PLEN
    me = lax.axis_index("dp")
    my_f = lax.axis_index("fsdp")
    dp_peers = [{"dp": lax.rem(me + off, n_dp)} for off in range(1, n_dp)]
    f_peers = [{"fsdp": lax.rem(my_f + off, n_f)} for off in range(1, n_f)]
    ready = greet(dp_peers + f_peers)
    gain = gain_ref[...].reshape(1, D)
    fgain = fgain_ref[...].reshape(1, D)

    shard = gout_ref.shape[0]
    rows_in = qkvw_ref.shape[0]
    first_row = 0 if gathered else pl.multiple_of(my_f * shard, 16)
    own_rows = pl.ds(first_row, rows_in)
    x_copy = pltpu.make_async_copy(x_hbm, x_ref, l_sem.at[0])
    w_copies = []
    for g in range(GROUPS):
        for part in range(3):
            copy = pltpu.make_async_copy(
                qkvw_ref.at[:, pl.ds(part * D + g * GW, GW)],
                w_ref.at[own_rows, pl.ds((g * 3 + part) * GW, GW)],
                l_sem.at[3 + g * 3 + part],
            )
            copy.start()
            w_copies.append(copy)
    oh_copies = [
        pltpu.make_async_copy(outw_hbm, outw_ref.at[own_rows, :], l_sem.at[1]),
        pltpu.make_async_copy(headw_hbm, headw_ref.at[own_rows, :], l_sem.at[2]),
    ]
    x_copy.start()
    for copy in oh_copies:
        copy.start()

    q_count = quer_ref.shape[0]
    mine[0:q_count, :] = quer_ref[...]
    row = lax.broadcasted_iota(jnp.int32, (16, CDIM), 0)
    lens = jnp.zeros((16, CDIM), F32)
    for a in range(passages):
        lens = jnp.where(row == a, qlen_ref[a].astype(F32), lens)
    mine[q_count : q_count + 16, :] = lens.astype(BF16)
    ready()

    pending = []
    steps = GROUPS + 1
    a_all, b_all, c_all = [None] * steps, [None] * steps, [None] * steps
    if not gathered:
        a_sems, b_sems, c_sems = sems[13:15], sems[15:17], sems[17:19]
        halves = n_dp // 2
        part = shard // halves
        h, c = me // 2, lax.rem(me, 2)
        sibling = {"dp": 2 * h + 1 - c}

        def block(i, f, hh):
            ref, base = (w_ref, i * 3 * GW) if i < GROUPS else (outw_ref, 0)
            width = 3 * GW // 2
            rows = pl.ds(pl.multiple_of(f * shard + hh * part, 16), part)
            return ref.at[rows, pl.ds(pl.multiple_of(base + c * width, 128), width)]

        def start_a(i):
            copies = []
            for k in range(1, n_f):
                piece = headw_ref.at[own_rows, :] if i == steps else block(i, my_f, h)
                copies.append(send(piece, piece, a_sems, i * (n_f - 1) + k - 1, f_peers[k - 1]))
            pending.extend(copies)
            return copies

        def from_f(k):
            return lax.rem(my_f + n_f - k, n_f)

        def from_h(j):
            return lax.rem(h + halves - j, halves)

        def at_b(i, k, j):
            return (i * (n_f - 1) + k - 1) * halves + j

    def spread(i):
        if gathered:
            return
        b_copies, c_copies = [], []
        for k in range(1, n_f):
            a_all[i][k - 1].wait_recv()
            piece = block(i, from_f(k), h)
            for j in range(1, halves):
                peer = {"dp": 2 * lax.rem(h + j, halves) + c}
                b_copies.append((k, j, send(piece, piece, b_sems, at_b(i, k, j), peer)))
            c_copies.append(send(piece, piece, c_sems, at_b(i, k, 0), sibling))
        pending.extend([copy for _, _, copy in b_copies])
        b_all[i], c_all[i] = b_copies, c_copies

    def share(i):
        if gathered:
            return
        for k, j, copy in b_all[i]:
            copy.wait_recv()
            piece = block(i, from_f(k), from_h(j))
            c_all[i].append(send(piece, piece, c_sems, at_b(i, k, j), sibling))
        pending.extend(c_all[i])

    def arrive(i):
        if gathered:
            return
        for copy in c_all[i]:
            copy.wait_recv()

    for g in range(GROUPS):
        for copy in w_copies[3 * g : 3 * g + 3]:
            copy.wait()
        if not gathered:
            a_all[g] = start_a(g)
    for copy in oh_copies:
        copy.wait()
    if not gathered:
        a_all[GROUPS] = start_a(GROUPS)
        a_head = start_a(steps)
    q_copies = [
        send(mine, pack_ref.at[me], q_sems, off, dp_peers[off]) for off in range(n_dp - 1)
    ]
    pending.extend(q_copies)
    pack_ref[me] = mine[...]
    x_copy.wait()
    spread(0)
    spread(1)

    def norm_rows_in(rows):
        n, _ = stats(x_ref[rows, :].astype(F32))
        normed[rows, :] = (n * gain).astype(BF16)

    row_loop(rows_all, norm_rows_in)
    share(0)
    spread(2)
    fill_bias(len_ref, bias, passages)
    low, keeps = half_masks()

    def project(g):
        for part in range(3):
            cols = slice((g * 3 + part) * GW, (g * 3 + part + 1) * GW)
            rows = dot_nn(normed[...], w_ref[:, cols])
            if part == 0:
                rows = rows * HD**-0.5
            qkv_ref[:, cols] = rows.astype(BF16)

    def attend(g):
        def pair(it, carry):
            p, w = it // (GW // 128), lax.rem(it, GW // 128)
            rows = pl.ds(pl.multiple_of(p * PLEN, PLEN), PLEN)
            at = head_at(g, w)
            q2 = qkv_ref[rows, pl.ds(at, 128)]
            k2 = qkv_ref[rows, pl.ds(at + GW, 128)]
            v2 = qkv_ref[rows, pl.ds(at + 2 * GW, 128)]
            outs = []
            for side, keep in enumerate(keeps):
                probs = probs_of(q2 * keep, k2, bias[p])
                saved[(p * (HEADS // 2) + g * (GW // 128) + w) * 2 + side] = probs
                outs.append(dot_tn(probs.astype(BF16), v2))
            out_at = pl.multiple_of(g * GW + w * 128, 128)
            ctx_ref[rows, pl.ds(out_at, 128)] = jnp.where(low, outs[0], outs[1]).astype(BF16)
            return carry

        lax.fori_loop(0, passages * (GW // 128), pair, 0)

    arrive(0)
    project(0)
    share(1)
    attend(0)
    spread(GROUPS)
    arrive(1)
    project(1)
    share(2)
    attend(1)
    arrive(2)
    project(2)
    share(GROUPS)
    attend(2)
    arrive(GROUPS)
    if not gathered:
        for copy in a_head:
            copy.wait_recv()
    for copy in q_copies:
        copy.wait_recv()

    def out_project(n, cols):
        res[:, cols] = x_ref[:, cols].astype(F32) + dot_nn(ctx_ref[...], outw_ref[:, cols])

    block_loop(D, out_project)

    def norm_rows(rows):
        n, inv = stats(res[rows, :])
        res[rows, :] = n
        inv_res[rows, :] = inv
        pooled[rows, :] = (n * fgain).astype(BF16)

    row_loop(rows_all, norm_rows)
    emb[...] = dot_nn(pooled[...], headw_ref[...])
    embedded = emb[...]
    inv_len = lax.rsqrt(jnp.sum(embedded * embedded, axis=-1, keepdims=True) + vec_eps)
    vectors = (embedded * inv_len).astype(BF16)
    q_near = passages * QLEN
    target = partner_ref[me]
    source = jnp.int32(0)
    for d in range(n_dp):
        source = jnp.where(partner_ref[d] == me, d, source)
    packs = (pack_ref[me], pack_ref[source])
    qf = jnp.concatenate([pack[:q_near].astype(F32) for pack in packs], axis=0)
    token = lax.broadcasted_iota(jnp.int32, (QLEN, CDIM), 0).astype(F32)
    masks = []
    for pack in packs:
        lens = pack[q_near : q_near + 16].astype(F32)
        for a in range(passages):
            masks.append(jnp.where(token < lens[a : a + 1], 1.0, 0.0))
    qmask = jnp.concatenate(masks, axis=0)[:, 0:1]
    qv = (qf * lax.rsqrt(jnp.sum(qf * qf, axis=-1, keepdims=True) + vec_eps)).astype(BF16)
    slot = lax.broadcasted_iota(jnp.int32, (1, PLEN), 1)
    live = jnp.concatenate(
        [jnp.where(slot < len_ref[b], 1.0, 0.0) for b in range(passages)], axis=1
    )
    weight = jnp.exp(dot_nt(qv, vectors) * (1.0 / soft_temp)) * live
    dens = [
        jnp.sum(weight[:, b * PLEN : (b + 1) * PLEN], axis=-1, keepdims=True)
        for b in range(passages)
    ]
    terms = [qmask * soft_temp * jnp.log(den) for den in dens]
    for q in range(2 * passages):
        for b in range(passages):
            total = jnp.sum(terms[b][q * QLEN : (q + 1) * QLEN], axis=0, keepdims=True)
            tile[q * passages + b : q * passages + b + 1, :] = jnp.broadcast_to(total, (1, 128))

    m_copies = [send(tile, got.at[me], m_sems, off, dp_peers[off]) for off in range(n_dp - 1)]
    got[me] = tile[...]
    for copy in m_copies:
        copy.wait()
    own = tile[...]
    from_target = got[target]
    from_source = got[source]
    half = passages * passages

    def logits_of(local, far, a):
        parts = [local[a * passages + b : a * passages + b + 1] for b in range(passages)]
        parts += [
            far[half + a * passages + b : half + a * passages + b + 1] for b in range(passages)
        ]
        total = jnp.exp(parts[0])
        for part in parts[1:]:
            total = total + jnp.exp(part)
        return parts, jnp.log(total)

    coef = [[] for _ in range(passages)]
    loss_ref[...] = jnp.zeros_like(loss_ref)
    for a in range(passages):
        parts, log_total = logits_of(own, from_target, a)
        loss_ref[a : a + 1, :] = log_total - parts[a]
        for b in range(passages):
            grad = jnp.exp(parts[b] - log_total) - (1.0 if a == b else 0.0)
            coef[b].append(jnp.broadcast_to(grad, (QLEN, 128)))
    for a in range(passages):
        parts, log_total = logits_of(from_source, own, a)
        for b in range(passages):
            grad = jnp.exp(parts[passages + b] - log_total)
            coef[b].append(jnp.broadcast_to(grad, (QLEN, 128)))
    for b in range(passages):
        rows = slice(b * PLEN, (b + 1) * PLEN)
        factor = jnp.concatenate(coef[b], axis=0)[:, 0:1] * qmask / dens[b]
        sim_grad = (weight[:, rows] * factor).astype(BF16)
        near = dot_tn(sim_grad[:q_near], qv[:q_near])
        far = dot_tn(sim_grad[q_near:], qv[q_near:]).astype(BF16).astype(F32)
        vgrad = near + far
        e, il = embedded[rows], inv_len[rows]
        along = jnp.sum(e * vgrad, axis=-1, keepdims=True)
        emb[rows, :] = il * vgrad - e * (il * il * il) * along
    emb_grad = emb[...].astype(BF16)
    wgrad_ref[:, D:] = dot_tn(pooled[...], emb_grad)

    def pool_back(n, cols):
        rg_ref[:, cols] = dot_nt(emb_grad, headw_ref[cols, :])

    block_loop(D, pool_back)

    def norm_back(rows):
        s = rg_ref[rows, :] * fgain
        n = res[rows, :]
        grad = inv_res[rows, :] * (
            s
            - jnp.mean(s, axis=-1, keepdims=True)
            - n * jnp.mean(s * n, axis=-1, keepdims=True)
        )
        rg_ref[rows, :] = grad
        rgb[rows, :] = grad.astype(BF16)

    row_loop(rows_all, norm_back)

    def out_back(n, cols):
        wgrad_ref[cols, :D] = dot_tn(ctx_ref[:, cols], rgb[...])

    block_loop(D, out_back)

    thin = s3.shape[0]
    used = shard // thin
    for d in range(n_dp):
        for f in range(n_f):
            if d < used:
                piece = wgrad_ref[f * shard + d * thin : f * shard + (d + 1) * thin, :]
                stage[d, f] = piece.astype(BF16)
            else:
                stage[d, f] = jnp.zeros(stage.shape[2:], BF16)
    quads = n_dp // 2
    my_h, my_c = me // 2, lax.rem(me, 2)
    g0 = [
        send(stage.at[2 * hh + 1 - my_c], r0.at[hh], g0_sems, hh, {"dp": 2 * my_h + 1 - my_c})
        for hh in range(quads)
    ]

    def context_back(n, cols):
        dctx_ref[:, cols] = dot_nt(rgb[...], outw_ref[cols, :]).astype(BF16)

    block_loop(D, context_back)

    def heads(p, first, last):
        rows = slice(p * PLEN, (p + 1) * PLEN)

        def pair(hp, carry):
            at = head_at(hp // (GW // 128), lax.rem(hp, GW // 128))
            q2 = qkv_ref[rows, pl.ds(at, 128)]
            k2 = qkv_ref[rows, pl.ds(at + GW, 128)]
            v2 = qkv_ref[rows, pl.ds(at + 2 * GW, 128)]
            d2 = dctx_ref[rows, pl.ds(pl.multiple_of(hp * 128, 128), 128)]
            qg, kg, vg = [], [], []
            for side, keep in enumerate(keeps):
                probs = saved[(p * (HEADS // 2) + hp) * 2 + side]
                prob_grad = dot_nt(v2, d2 * keep)
                vg.append(dot_nn(probs.astype(BF16), d2))
                inner = jnp.sum(probs * prob_grad, axis=0, keepdims=True)
                score_grad = (probs * (prob_grad - inner)).astype(BF16)
                qg.append(dot_tn(score_grad, k2))
                kg.append(dot_nn(score_grad, q2))
            grads[rows, pl.ds(at, 128)] = (jnp.where(low, qg[0], qg[1]) * HD**-0.5).astype(BF16)
            grads[rows, pl.ds(at + GW, 128)] = jnp.where(low, kg[0], kg[1]).astype(BF16)
            grads[rows, pl.ds(at + 2 * GW, 128)] = jnp.where(low, vg[0], vg[1]).astype(BF16)
            return carry

        lax.fori_loop(first, last, pair, 0)

    pairs = HEADS // 2
    heads(0, 0, 1)
    for copy in g0:
        copy.wait_recv()
    for hh in range(quads):
        for f in range(n_f):
            both = stage[2 * hh + my_c, f].astype(F32) + r0[hh, f].astype(F32)
            pre[hh, f] = both.astype(BF16)
    g1 = [
        send(
            pre.at[lax.rem(my_h + off, quads)],
            r1.at[my_h],
            g1_sems,
            off - 1,
            {"dp": 2 * lax.rem(my_h + off, quads) + my_c},
        )
        for off in range(1, quads)
    ]
    heads(0, 1, pairs)
    for p in range(1, passages - 1):
        heads(p, 0, pairs)
    heads(passages - 1, 0, pairs - 2)

    for copy in g1:
        copy.wait_recv()
    for f in range(n_f):
        total = pre[my_h, f].astype(F32)
        for off in range(1, quads):
            total = total + r1[lax.rem(my_h + off, quads), f].astype(F32)
        acc[f] = total
        s2[f] = total.astype(BF16)
    g2 = [
        send(s2.at[lax.rem(my_f + off, n_f)], r2.at[my_f], g2_sems, off - 1, f_peers[off - 1])
        for off in range(1, n_f)
    ]
    heads(passages - 1, pairs - 2, pairs)
    for copy in g2:
        copy.wait_recv()
    total = acc[my_f]
    for off in range(1, n_f):
        total = total + r2[lax.rem(my_f + off, n_f)].astype(F32)
    s3[...] = total.astype(BF16)
    g3 = [send(s3, r3.at[me], g3_sems, off, dp_peers[off]) for off in range(n_dp - 1)]
    r3[me] = s3[...]

    def project_back(n, cols):
        res[:, cols] = dot_nt(grads[...], w_ref[cols, :])

    block_loop(D, project_back)

    def norm_back_in(rows):
        n, inv = stats(x_ref[rows, :].astype(F32))
        t = res[rows, :] * gain
        grad = inv * (
            t
            - jnp.mean(t, axis=-1, keepdims=True)
            - n * jnp.mean(t * n, axis=-1, keepdims=True)
        )
        gin_ref[rows, :] = (rg_ref[rows, :] + grad).astype(BF16)

    row_loop(rows_all, norm_back_in)
    for copy in g3:
        copy.wait_recv()
    for d in range(used):
        piece = r3[d].astype(F32)
        gout_ref[d * thin : (d + 1) * thin, :] = piece[:, :D]
        ghead_ref[d * thin : (d + 1) * thin, :] = piece[:, D:]
    for copy in pending + g0 + g1 + g2 + g3:
        copy.wait_send()


def finish_kernel(gin, gout, ghead, loss, gin_out, gout_out, ghead_out, loss_out, sems):
    copies = [
        pltpu.make_async_copy(source, target, sems.at[i])
        for i, (source, target) in enumerate(
            ((gin, gin_out), (gout, gout_out), (ghead, ghead_out))
        )
    ]
    for copy in copies:
        copy.start()
    for a in range(loss_out.shape[0]):
        loss_out[a] = jnp.max(loss[a : a + 1, :])
    for copy in copies:
        copy.wait()


VM = pl.BlockSpec(memory_space=pltpu.VMEM)
SM = pl.BlockSpec(memory_space=pltpu.SMEM)
HB = pl.BlockSpec(memory_space=pl.ANY)
VMEM_LIMIT = 56 << 20


def sem_pair(count):
    return [pltpu.SemaphoreType.DMA((count,))] * 2


def per_device(
    n_dp,
    n_f,
    hidden_in,
    norm_gain,
    qkv_weight,
    out_weight,
    final_gain,
    head_weight,
    queries,
    query_lengths,
    passage_lengths,
    partner,
):
    tok = hidden_in.shape[0]
    count = passage_lengths.shape[0]
    qrows = count * QLEN
    shape = jax.ShapeDtypeStruct
    shard = qkv_weight.shape[0]
    weights = (qkv_weight, out_weight, head_weight)
    gathered = n_dp % 2 != 0 or shard % (8 * n_dp) != 0
    if gathered:
        weights = tuple(lax.all_gather(w, "fsdp", axis=0, tiled=True) for w in weights)
    copies = (n_f - 1) * n_dp // 2
    steps = GROUPS + 1
    extra = (
        []
        if gathered
        else sem_pair((steps + 1) * (n_f - 1))
        + sem_pair(steps * copies)
        + sem_pair(steps * copies)
    )
    thin = -(-shard // (8 * n_dp)) * 8
    wide = D + CDIM
    held = pl.pallas_call(
        functools.partial(step_kernel, n_dp, n_f, gathered),
        out_shape=(
            pltpu.VMEM((tok, D), BF16),
            pltpu.VMEM((shard, D), F32),
            pltpu.VMEM((shard, CDIM), F32),
            pltpu.VMEM((8, 128), F32),
        ),
        in_specs=[HB, SM, SM, SM, VM, VM, VM, HB, HB, HB],
        out_specs=(VM,) * 4,
        scratch_shapes=[
            pltpu.VMEM((tok, D), BF16),
            pltpu.VMEM((D, 3 * D), BF16),
            pltpu.VMEM((D, D), BF16),
            pltpu.VMEM((D, CDIM), BF16),
            pltpu.VMEM((tok, 3 * D), BF16),
            pltpu.VMEM((tok, D), BF16),
            pltpu.VMEM((n_dp, qrows + 16, CDIM), BF16),
            pltpu.VMEM((tok, D), BF16),
            pltpu.VMEM((qrows + 16, CDIM), BF16),
            pltpu.VMEM((tok, D), F32),
            pltpu.VMEM((tok, 1), F32),
            pltpu.VMEM((tok, D), BF16),
            pltpu.VMEM((tok, CDIM), F32),
            pltpu.VMEM((tok, D), BF16),
            pltpu.VMEM((tok, D), F32),
            pltpu.VMEM((tok, D), BF16),
            pltpu.VMEM((D, wide), F32),
            pltpu.VMEM((tok, 3 * D), BF16),
            pltpu.VMEM((count, PLEN, PLEN), F32),
            pltpu.VMEM((count * HEADS, PLEN, PLEN), F32),
            pltpu.VMEM((2 * count * count, 128), F32),
            pltpu.VMEM((n_dp, 2 * count * count, 128), F32),
            pltpu.VMEM((n_dp, n_f, thin, wide), BF16),
            pltpu.VMEM((n_dp // 2, n_f, thin, wide), BF16),
            pltpu.VMEM((n_dp // 2, n_f, thin, wide), BF16),
            pltpu.VMEM((n_dp // 2, n_f, thin, wide), BF16),
            pltpu.VMEM((n_f, thin, wide), F32),
            pltpu.VMEM((n_f, thin, wide), BF16),
            pltpu.VMEM((n_f, thin, wide), BF16),
            pltpu.VMEM((thin, wide), BF16),
            pltpu.VMEM((n_dp, thin, wide), BF16),
        ]
        + sem_pair(n_dp - 1)
        + sem_pair(n_dp - 1)
        + sem_pair(n_dp // 2)
        + sem_pair(n_dp // 2 - 1)
        + sem_pair(n_f - 1)
        + sem_pair(n_dp - 1)
        + [pltpu.SemaphoreType.DMA((3 + 3 * GROUPS,))]
        + extra,
        compiler_params=pltpu.CompilerParams(
            vmem_limit_bytes=VMEM_LIMIT, collective_id=1, has_side_effects=True
        ),
        name="step",
    )(
        hidden_in,
        passage_lengths,
        query_lengths,
        partner,
        norm_gain,
        final_gain,
        queries.reshape(qrows, CDIM),
        *weights,
    )
    grad_input, grad_out, grad_head, losses = pl.pallas_call(
        finish_kernel,
        out_shape=(
            shape((tok, D), BF16),
            shape((shard, D), F32),
            shape((shard, CDIM), F32),
            shape((count,), F32),
        ),
        in_specs=[VM] * 4,
        out_specs=(HB, HB, HB, SM),
        scratch_shapes=[pltpu.SemaphoreType.DMA((3,))],
        compiler_params=pltpu.CompilerParams(vmem_limit_bytes=4 << 20),
        name="finish",
    )(*[pltpu.with_memory_space_constraint(a, pltpu.VMEM) for a in held])
    return losses, grad_input, grad_out, grad_head


def solution(mesh):
    placed = (
        P(("dp", "fsdp"), None),
        P(),
        P("fsdp", None),
        P("fsdp", None),
        P(),
        P("fsdp", None),
        P(("dp", "fsdp"), None, None),
        P(("dp", "fsdp")),
        P(("dp", "fsdp")),
        P(),
    )
    return jax.shard_map(
        functools.partial(per_device, mesh.shape["dp"], mesh.shape["fsdp"]),
        mesh=mesh,
        in_specs=placed,
        out_specs=(P(("dp", "fsdp")), P(("dp", "fsdp"), None), P("fsdp", None), P("fsdp", None)),
        check_vma=False,
    )
```

```python
import functools

import jax
import jax.numpy as jnp
from jax import lax
from jax.experimental import pallas as pl
from jax.experimental.pallas import tpu as pltpu
from jax.sharding import PartitionSpec as P

D = 768
HEADS = 12
HD = D // HEADS
CDIM = 128
WIN = 64
PLEN = 256
QLEN = 32
NB = 256
QB = 128
KB = QB + WIN
SPANS = PLEN // QB
UNROLL = 2
RB = 128

norm_eps = 1e-05
vec_eps = 1e-06
soft_temp = 0.05
masked_fill = -1e30

MESH = pl.DeviceIdType.MESH
F32 = jnp.float32
BF16 = jnp.bfloat16


def dot_nn(a, b):
    return lax.dot_general(a, b, (((1,), (0,)), ((), ())), preferred_element_type=F32)


def dot_nt(a, b):
    return lax.dot_general(a, b, (((1,), (1,)), ((), ())), preferred_element_type=F32)


def dot_tn(a, b):
    return lax.dot_general(a, b, (((0,), (0,)), ((), ())), preferred_element_type=F32)


def stats(rows):
    centered = rows - jnp.mean(rows, axis=-1, keepdims=True)
    inv_std = lax.rsqrt(jnp.mean(centered * centered, axis=-1, keepdims=True) + norm_eps)
    return centered * inv_std, inv_std


def row_loop(count, body):
    def step(i, carry):
        body(pl.ds(pl.multiple_of(i * RB, RB), RB))
        return carry

    lax.fori_loop(0, count // RB, step, 0)


def block_loop(count, body):
    def step(n, carry):
        body(n, pl.ds(pl.multiple_of(n * NB, NB), NB))
        return carry

    lax.fori_loop(0, count // NB, step, 0)


def fill_bias(len_ref, bias, passages):
    for b in range(SPANS):
        key = lax.broadcasted_iota(jnp.int32, (KB, QB), 0) + b * WIN
        query = lax.broadcasted_iota(jnp.int32, (KB, QB), 1) + b * QB
        in_band = jnp.abs(key - query) <= WIN
        for p in range(passages):
            allowed = in_band & ((key < len_ref[p]) | (key == query))
            bias[p * SPANS + b] = jnp.where(allowed, 0.0, masked_fill)


def half_masks():
    lane = lax.broadcasted_iota(jnp.int32, (QB, 128), 1)
    low = lane < HD
    keep = jnp.where(low, 1.0, 0.0)
    return low, (keep.astype(BF16), (1.0 - keep).astype(BF16))


def probs_of(scores):
    shifted = jnp.exp(scores - jnp.max(scores, axis=0, keepdims=True))
    return shifted * (1.0 / jnp.sum(shifted, axis=0, keepdims=True))


def greet(peers):
    barrier = pltpu.get_barrier_semaphore()
    for peer in peers:
        pl.semaphore_signal(barrier, inc=1, device_id=peer, device_id_type=MESH)
    return lambda: pl.semaphore_wait(barrier, len(peers))


def send(src, dst, sems, at, peer):
    copy = pltpu.make_async_remote_copy(
        src_ref=src,
        dst_ref=dst,
        send_sem=sems[0].at[at],
        recv_sem=sems[1].at[at],
        device_id=peer,
        device_id_type=MESH,
    )
    copy.start()
    return copy


GROUPS = 3
GW = D // GROUPS


def head_at(g, w):
    return pl.multiple_of(g * 3 * GW + w * 128, 128)


def step_kernel(
    n_dp,
    n_f,
    gathered,
    x_hbm,
    len_ref,
    qlen_ref,
    partner_ref,
    gain_ref,
    fgain_ref,
    quer_ref,
    qkvw_ref,
    outw_hbm,
    headw_hbm,
    gin_ref,
    gout_ref,
    ghead_ref,
    loss_ref,
    x_ref,
    w_ref,
    outw_ref,
    headw_ref,
    qkv_ref,
    ctx_ref,
    pack_ref,
    normed,
    mine,
    res,
    inv_res,
    pooled,
    emb,
    rgb,
    rg_ref,
    dctx_ref,
    wgrad_ref,
    grads,
    bias,
    saved,
    tile,
    got,
    stage,
    r0,
    pre,
    r1,
    acc,
    s2,
    r2,
    s3,
    r3,
    *sems,
):
    q_sems, m_sems, g0_sems, g1_sems, g2_sems, g3_sems = [
        sems[2 * i : 2 * i + 2] for i in range(6)
    ]
    l_sem = sems[12]
    rows_all = x_ref.shape[0]
    passages = rows_all // PLEN
    me = lax.axis_index("dp")
    my_f = lax.axis_index("fsdp")
    dp_peers = [{"dp": lax.rem(me + off, n_dp)} for off in range(1, n_dp)]
    f_peers = [{"fsdp": lax.rem(my_f + off, n_f)} for off in range(1, n_f)]
    ready = greet(dp_peers + f_peers)
    gain = gain_ref[...].reshape(1, D)
    fgain = fgain_ref[...].reshape(1, D)

    shard = gout_ref.shape[0]
    rows_in = qkvw_ref.shape[0]
    first_row = 0 if gathered else pl.multiple_of(my_f * shard, 16)
    own_rows = pl.ds(first_row, rows_in)
    x_copy = pltpu.make_async_copy(x_hbm, x_ref, l_sem.at[0])
    w_copies = []
    for g in range(GROUPS):
        for part in range(3):
            copy = pltpu.make_async_copy(
                qkvw_ref.at[:, pl.ds(part * D + g * GW, GW)],
                w_ref.at[own_rows, pl.ds((g * 3 + part) * GW, GW)],
                l_sem.at[3 + g * 3 + part],
            )
            copy.start()
            w_copies.append(copy)
    oh_copies = [
        pltpu.make_async_copy(outw_hbm, outw_ref.at[own_rows, :], l_sem.at[1]),
        pltpu.make_async_copy(headw_hbm, headw_ref.at[own_rows, :], l_sem.at[2]),
    ]
    x_copy.start()
    for copy in oh_copies:
        copy.start()

    q_count = quer_ref.shape[0]
    mine[0:q_count, :] = quer_ref[...]
    row = lax.broadcasted_iota(jnp.int32, (16, CDIM), 0)
    lens = jnp.zeros((16, CDIM), F32)
    for a in range(passages):
        lens = jnp.where(row == a, qlen_ref[a].astype(F32), lens)
    mine[q_count : q_count + 16, :] = lens.astype(BF16)
    ready()

    pending = []
    steps = GROUPS + 1
    a_all, b_all, c_all = [None] * steps, [None] * steps, [None] * steps
    if not gathered:
        a_sems, b_sems, c_sems = sems[13:15], sems[15:17], sems[17:19]
        halves = n_dp // 2
        part = shard // halves
        h, c = me // 2, lax.rem(me, 2)
        sibling = {"dp": 2 * h + 1 - c}

        def block(i, f, hh):
            ref, base = (w_ref, i * 3 * GW) if i < GROUPS else (outw_ref, 0)
            width = 3 * GW // 2
            rows = pl.ds(pl.multiple_of(f * shard + hh * part, 16), part)
            return ref.at[rows, pl.ds(pl.multiple_of(base + c * width, 128), width)]

        def start_a(i):
            copies = []
            for k in range(1, n_f):
                piece = headw_ref.at[own_rows, :] if i == steps else block(i, my_f, h)
                copies.append(send(piece, piece, a_sems, i * (n_f - 1) + k - 1, f_peers[k - 1]))
            pending.extend(copies)
            return copies

        def from_f(k):
            return lax.rem(my_f + n_f - k, n_f)

        def from_h(j):
            return lax.rem(h + halves - j, halves)

        def at_b(i, k, j):
            return (i * (n_f - 1) + k - 1) * halves + j

    def spread(i):
        if gathered:
            return
        b_copies, c_copies = [], []
        for k in range(1, n_f):
            a_all[i][k - 1].wait_recv()
            piece = block(i, from_f(k), h)
            for j in range(1, halves):
                peer = {"dp": 2 * lax.rem(h + j, halves) + c}
                b_copies.append((k, j, send(piece, piece, b_sems, at_b(i, k, j), peer)))
            c_copies.append(send(piece, piece, c_sems, at_b(i, k, 0), sibling))
        pending.extend([copy for _, _, copy in b_copies])
        b_all[i], c_all[i] = b_copies, c_copies

    def share(i):
        if gathered:
            return
        for k, j, copy in b_all[i]:
            copy.wait_recv()
            piece = block(i, from_f(k), from_h(j))
            c_all[i].append(send(piece, piece, c_sems, at_b(i, k, j), sibling))
        pending.extend(c_all[i])

    def arrive(i):
        if gathered:
            return
        for copy in c_all[i]:
            copy.wait_recv()

    for g in range(GROUPS):
        for copy in w_copies[3 * g : 3 * g + 3]:
            copy.wait()
        if not gathered:
            a_all[g] = start_a(g)
    for copy in oh_copies:
        copy.wait()
    if not gathered:
        a_all[GROUPS] = start_a(GROUPS)
        a_head = start_a(steps)
    q_copies = [
        send(mine, pack_ref.at[me], q_sems, off, dp_peers[off]) for off in range(n_dp - 1)
    ]
    pending.extend(q_copies)
    pack_ref[me] = mine[...]
    x_copy.wait()
    spread(0)
    spread(1)

    def norm_rows_in(rows):
        n, _ = stats(x_ref[rows, :].astype(F32))
        normed[rows, :] = (n * gain).astype(BF16)

    row_loop(rows_all, norm_rows_in)
    share(0)
    spread(2)
    fill_bias(len_ref, bias, passages)
    low, keeps = half_masks()

    def sides(rows):
        return jnp.concatenate([rows * keeps[0], rows * keeps[1]], axis=0)

    def spans(p, b):
        queries = pl.ds(pl.multiple_of(p * PLEN + b * QB, QB), QB)
        keys = pl.ds(pl.multiple_of(p * PLEN + b * WIN, WIN), KB)
        return queries, keys

    def project(g):
        for part in range(3):
            cols = slice((g * 3 + part) * GW, (g * 3 + part + 1) * GW)
            rows = dot_nn(normed[...], w_ref[:, cols])
            if part == 0:
                rows = rows * HD**-0.5
            qkv_ref[:, cols] = rows.astype(BF16)

    def attend(g):
        def pair(it, carry):
            p, w = it // (GW // 128), lax.rem(it, GW // 128)
            at = head_at(g, w)
            out_at = pl.multiple_of(g * GW + w * 128, 128)
            slot = (p * (HEADS // 2) + g * (GW // 128) + w) * SPANS
            for b in range(SPANS):
                qrows, krows = spans(p, b)
                scores = dot_nt(
                    qkv_ref[krows, pl.ds(at + GW, 128)], sides(qkv_ref[qrows, pl.ds(at, 128)])
                )
                both = []
                for side in range(2):
                    lanes = slice(side * QB, (side + 1) * QB)
                    probs = probs_of(scores[:, lanes] + bias[p * SPANS + b])
                    saved[slot + b, :, lanes] = probs
                    both.append(probs.astype(BF16))
                out = dot_tn(jnp.concatenate(both, axis=1), qkv_ref[krows, pl.ds(at + 2 * GW, 128)])
                ctx_ref[qrows, pl.ds(out_at, 128)] = jnp.where(low, out[:QB], out[QB:]).astype(BF16)
            return carry

        lax.fori_loop(0, passages * (GW // 128), pair, 0, unroll=UNROLL)

    arrive(0)
    project(0)
    share(1)
    attend(0)
    spread(GROUPS)
    arrive(1)
    project(1)
    share(2)
    attend(1)
    arrive(2)
    project(2)
    share(GROUPS)
    attend(2)
    arrive(GROUPS)
    if not gathered:
        for copy in a_head:
            copy.wait_recv()
    for copy in q_copies:
        copy.wait_recv()

    def out_project(n, cols):
        res[:, cols] = x_ref[:, cols].astype(F32) + dot_nn(ctx_ref[...], outw_ref[:, cols])

    block_loop(D, out_project)

    def norm_rows(rows):
        n, inv = stats(res[rows, :])
        res[rows, :] = n
        inv_res[rows, :] = inv
        pooled[rows, :] = (n * fgain).astype(BF16)

    row_loop(rows_all, norm_rows)
    emb[...] = dot_nn(pooled[...], headw_ref[...])
    embedded = emb[...]
    inv_len = lax.rsqrt(jnp.sum(embedded * embedded, axis=-1, keepdims=True) + vec_eps)
    vectors = (embedded * inv_len).astype(BF16)
    q_near = passages * QLEN
    target = partner_ref[me]
    source = jnp.int32(0)
    for d in range(n_dp):
        source = jnp.where(partner_ref[d] == me, d, source)
    packs = (pack_ref[me], pack_ref[source])
    qf = jnp.concatenate([pack[:q_near].astype(F32) for pack in packs], axis=0)
    token = lax.broadcasted_iota(jnp.int32, (QLEN, CDIM), 0).astype(F32)
    masks = []
    for pack in packs:
        lens = pack[q_near : q_near + 16].astype(F32)
        for a in range(passages):
            masks.append(jnp.where(token < lens[a : a + 1], 1.0, 0.0))
    qmask = jnp.concatenate(masks, axis=0)[:, 0:1]
    qv = (qf * lax.rsqrt(jnp.sum(qf * qf, axis=-1, keepdims=True) + vec_eps)).astype(BF16)
    slot = lax.broadcasted_iota(jnp.int32, (1, PLEN), 1)
    live = jnp.concatenate(
        [jnp.where(slot < len_ref[b], 1.0, 0.0) for b in range(passages)], axis=1
    )
    weight = jnp.exp(dot_nt(qv, vectors) * (1.0 / soft_temp)) * live
    dens = [
        jnp.sum(weight[:, b * PLEN : (b + 1) * PLEN], axis=-1, keepdims=True)
        for b in range(passages)
    ]
    terms = [qmask * soft_temp * jnp.log(den) for den in dens]
    for q in range(2 * passages):
        for b in range(passages):
            total = jnp.sum(terms[b][q * QLEN : (q + 1) * QLEN], axis=0, keepdims=True)
            tile[q * passages + b : q * passages + b + 1, :] = jnp.broadcast_to(total, (1, 128))

    m_copies = [send(tile, got.at[me], m_sems, off, dp_peers[off]) for off in range(n_dp - 1)]
    got[me] = tile[...]
    for copy in m_copies:
        copy.wait()
    own = tile[...]
    from_target = got[target]
    from_source = got[source]
    half = passages * passages

    def logits_of(local, far, a):
        parts = [local[a * passages + b : a * passages + b + 1] for b in range(passages)]
        parts += [
            far[half + a * passages + b : half + a * passages + b + 1] for b in range(passages)
        ]
        total = jnp.exp(parts[0])
        for part in parts[1:]:
            total = total + jnp.exp(part)
        return parts, jnp.log(total)

    coef = [[] for _ in range(passages)]
    loss_ref[...] = jnp.zeros_like(loss_ref)
    for a in range(passages):
        parts, log_total = logits_of(own, from_target, a)
        loss_ref[a : a + 1, :] = log_total - parts[a]
        for b in range(passages):
            grad = jnp.exp(parts[b] - log_total) - (1.0 if a == b else 0.0)
            coef[b].append(jnp.broadcast_to(grad, (QLEN, 128)))
    for a in range(passages):
        parts, log_total = logits_of(from_source, own, a)
        for b in range(passages):
            grad = jnp.exp(parts[passages + b] - log_total)
            coef[b].append(jnp.broadcast_to(grad, (QLEN, 128)))
    for b in range(passages):
        rows = slice(b * PLEN, (b + 1) * PLEN)
        factor = jnp.concatenate(coef[b], axis=0)[:, 0:1] * qmask / dens[b]
        sim_grad = (weight[:, rows] * factor).astype(BF16)
        near = dot_tn(sim_grad[:q_near], qv[:q_near])
        far = dot_tn(sim_grad[q_near:], qv[q_near:]).astype(BF16).astype(F32)
        vgrad = near + far
        e, il = embedded[rows], inv_len[rows]
        along = jnp.sum(e * vgrad, axis=-1, keepdims=True)
        emb[rows, :] = il * vgrad - e * (il * il * il) * along
    emb_grad = emb[...].astype(BF16)
    wgrad_ref[:, D:] = dot_tn(pooled[...], emb_grad)

    def pool_back(n, cols):
        rg_ref[:, cols] = dot_nt(emb_grad, headw_ref[cols, :])

    block_loop(D, pool_back)

    def norm_back(rows):
        s = rg_ref[rows, :] * fgain
        n = res[rows, :]
        grad = inv_res[rows, :] * (
            s
            - jnp.mean(s, axis=-1, keepdims=True)
            - n * jnp.mean(s * n, axis=-1, keepdims=True)
        )
        rg_ref[rows, :] = grad
        rgb[rows, :] = grad.astype(BF16)

    row_loop(rows_all, norm_back)

    def out_back(n, cols):
        wgrad_ref[cols, :D] = dot_tn(ctx_ref[:, cols], rgb[...])

    block_loop(D, out_back)

    thin = s3.shape[0]
    used = shard // thin
    for d in range(n_dp):
        for f in range(n_f):
            if d < used:
                piece = wgrad_ref[f * shard + d * thin : f * shard + (d + 1) * thin, :]
                stage[d, f] = piece.astype(BF16)
            else:
                stage[d, f] = jnp.zeros(stage.shape[2:], BF16)
    quads = n_dp // 2
    my_h, my_c = me // 2, lax.rem(me, 2)
    g0 = [
        send(stage.at[2 * hh + 1 - my_c], r0.at[hh], g0_sems, hh, {"dp": 2 * my_h + 1 - my_c})
        for hh in range(quads)
    ]

    def context_back(n, cols):
        dctx_ref[:, cols] = dot_nt(rgb[...], outw_ref[cols, :]).astype(BF16)

    block_loop(D, context_back)

    pairs = HEADS // 2

    def heads(first, last):
        def pair(it, carry):
            p, hp = it // pairs, lax.rem(it, pairs)
            at = head_at(hp // (GW // 128), lax.rem(hp, GW // 128))
            d_at = pl.multiple_of(hp * 128, 128)
            kg, vg = [], []
            for b in range(SPANS):
                qrows, krows = spans(p, b)
                q2 = sides(qkv_ref[qrows, pl.ds(at, 128)])
                d2 = sides(dctx_ref[qrows, pl.ds(d_at, 128)])
                k2 = qkv_ref[krows, pl.ds(at + GW, 128)]
                prob_grad = dot_nt(qkv_ref[krows, pl.ds(at + 2 * GW, 128)], d2)
                probs_b, score_b = [], []
                for side in range(2):
                    lanes = slice(side * QB, (side + 1) * QB)
                    probs, grad = saved[it * SPANS + b, :, lanes], prob_grad[:, lanes]
                    inner = jnp.sum(probs * grad, axis=0, keepdims=True)
                    probs_b.append(probs.astype(BF16))
                    score_b.append((probs * (grad - inner)).astype(BF16))
                score_grad = jnp.concatenate(score_b, axis=1)
                vg.append(dot_nn(jnp.concatenate(probs_b, axis=1), d2))
                kg.append(dot_nn(score_grad, q2))
                qg = dot_tn(score_grad, k2)
                qg = jnp.where(low, qg[:QB], qg[QB:]) * HD**-0.5
                grads[qrows, pl.ds(at, 128)] = qg.astype(BF16)
            rows = pl.ds(pl.multiple_of(p * PLEN, PLEN), PLEN)
            for offset, parts in ((GW, kg), (2 * GW, vg)):
                lower, upper = parts
                whole = jnp.concatenate(
                    [lower[:WIN], lower[WIN:] + upper[: KB - WIN], upper[KB - WIN :]], axis=0
                )
                grads[rows, pl.ds(at + offset, 128)] = whole.astype(BF16)
            return carry

        lax.fori_loop(first, last, pair, 0, unroll=UNROLL)

    heads(0, 2)
    for copy in g0:
        copy.wait_recv()
    for hh in range(quads):
        for f in range(n_f):
            both = stage[2 * hh + my_c, f].astype(F32) + r0[hh, f].astype(F32)
            pre[hh, f] = both.astype(BF16)
    g1 = [
        send(
            pre.at[lax.rem(my_h + off, quads)],
            r1.at[my_h],
            g1_sems,
            off - 1,
            {"dp": 2 * lax.rem(my_h + off, quads) + my_c},
        )
        for off in range(1, quads)
    ]
    heads(2, passages * pairs - 2)

    for copy in g1:
        copy.wait_recv()
    for f in range(n_f):
        total = pre[my_h, f].astype(F32)
        for off in range(1, quads):
            total = total + r1[lax.rem(my_h + off, quads), f].astype(F32)
        acc[f] = total
        s2[f] = total.astype(BF16)
    g2 = [
        send(s2.at[lax.rem(my_f + off, n_f)], r2.at[my_f], g2_sems, off - 1, f_peers[off - 1])
        for off in range(1, n_f)
    ]
    heads(passages * pairs - 2, passages * pairs)
    for copy in g2:
        copy.wait_recv()
    total = acc[my_f]
    for off in range(1, n_f):
        total = total + r2[lax.rem(my_f + off, n_f)].astype(F32)
    s3[...] = total.astype(BF16)
    g3 = [send(s3, r3.at[me], g3_sems, off, dp_peers[off]) for off in range(n_dp - 1)]
    r3[me] = s3[...]

    def project_back(n, cols):
        res[:, cols] = dot_nt(grads[...], w_ref[cols, :])

    block_loop(D, project_back)

    def norm_back_in(rows):
        n, inv = stats(x_ref[rows, :].astype(F32))
        t = res[rows, :] * gain
        grad = inv * (
            t
            - jnp.mean(t, axis=-1, keepdims=True)
            - n * jnp.mean(t * n, axis=-1, keepdims=True)
        )
        gin_ref[rows, :] = (rg_ref[rows, :] + grad).astype(BF16)

    row_loop(rows_all, norm_back_in)
    for copy in g3:
        copy.wait_recv()
    for d in range(used):
        piece = r3[d].astype(F32)
        gout_ref[d * thin : (d + 1) * thin, :] = piece[:, :D]
        ghead_ref[d * thin : (d + 1) * thin, :] = piece[:, D:]
    for copy in pending + g0 + g1 + g2 + g3:
        copy.wait_send()


def finish_kernel(gin, gout, ghead, loss, gin_out, gout_out, ghead_out, loss_out, sems):
    copies = [
        pltpu.make_async_copy(source, target, sems.at[i])
        for i, (source, target) in enumerate(
            ((gin, gin_out), (gout, gout_out), (ghead, ghead_out))
        )
    ]
    for copy in copies:
        copy.start()
    for a in range(loss_out.shape[0]):
        loss_out[a] = jnp.max(loss[a : a + 1, :])
    for copy in copies:
        copy.wait()


VM = pl.BlockSpec(memory_space=pltpu.VMEM)
SM = pl.BlockSpec(memory_space=pltpu.SMEM)
HB = pl.BlockSpec(memory_space=pl.ANY)
VMEM_LIMIT = 56 << 20


def sem_pair(count):
    return [pltpu.SemaphoreType.DMA((count,))] * 2


def per_device(
    n_dp,
    n_f,
    hidden_in,
    norm_gain,
    qkv_weight,
    out_weight,
    final_gain,
    head_weight,
    queries,
    query_lengths,
    passage_lengths,
    partner,
):
    tok = hidden_in.shape[0]
    count = passage_lengths.shape[0]
    qrows = count * QLEN
    shape = jax.ShapeDtypeStruct
    shard = qkv_weight.shape[0]
    weights = (qkv_weight, out_weight, head_weight)
    gathered = n_dp % 2 != 0 or shard % (8 * n_dp) != 0
    if gathered:
        weights = tuple(lax.all_gather(w, "fsdp", axis=0, tiled=True) for w in weights)
    copies = (n_f - 1) * n_dp // 2
    steps = GROUPS + 1
    extra = (
        []
        if gathered
        else sem_pair((steps + 1) * (n_f - 1))
        + sem_pair(steps * copies)
        + sem_pair(steps * copies)
    )
    thin = -(-shard // (8 * n_dp)) * 8
    wide = D + CDIM
    held = pl.pallas_call(
        functools.partial(step_kernel, n_dp, n_f, gathered),
        out_shape=(
            pltpu.VMEM((tok, D), BF16),
            pltpu.VMEM((shard, D), F32),
            pltpu.VMEM((shard, CDIM), F32),
            pltpu.VMEM((8, 128), F32),
        ),
        in_specs=[HB, SM, SM, SM, VM, VM, VM, HB, HB, HB],
        out_specs=(VM,) * 4,
        scratch_shapes=[
            pltpu.VMEM((tok, D), BF16),
            pltpu.VMEM((D, 3 * D), BF16),
            pltpu.VMEM((D, D), BF16),
            pltpu.VMEM((D, CDIM), BF16),
            pltpu.VMEM((tok, 3 * D), BF16),
            pltpu.VMEM((tok, D), BF16),
            pltpu.VMEM((n_dp, qrows + 16, CDIM), BF16),
            pltpu.VMEM((tok, D), BF16),
            pltpu.VMEM((qrows + 16, CDIM), BF16),
            pltpu.VMEM((tok, D), F32),
            pltpu.VMEM((tok, 1), F32),
            pltpu.VMEM((tok, D), BF16),
            pltpu.VMEM((tok, CDIM), F32),
            pltpu.VMEM((tok, D), BF16),
            pltpu.VMEM((tok, D), F32),
            pltpu.VMEM((tok, D), BF16),
            pltpu.VMEM((D, wide), F32),
            pltpu.VMEM((tok, 3 * D), BF16),
            pltpu.VMEM((count * SPANS, KB, QB), F32),
            pltpu.VMEM((count * (HEADS // 2) * SPANS, KB, 2 * QB), F32),
            pltpu.VMEM((2 * count * count, 128), F32),
            pltpu.VMEM((n_dp, 2 * count * count, 128), F32),
            pltpu.VMEM((n_dp, n_f, thin, wide), BF16),
            pltpu.VMEM((n_dp // 2, n_f, thin, wide), BF16),
            pltpu.VMEM((n_dp // 2, n_f, thin, wide), BF16),
            pltpu.VMEM((n_dp // 2, n_f, thin, wide), BF16),
            pltpu.VMEM((n_f, thin, wide), F32),
            pltpu.VMEM((n_f, thin, wide), BF16),
            pltpu.VMEM((n_f, thin, wide), BF16),
            pltpu.VMEM((thin, wide), BF16),
            pltpu.VMEM((n_dp, thin, wide), BF16),
        ]
        + sem_pair(n_dp - 1)
        + sem_pair(n_dp - 1)
        + sem_pair(n_dp // 2)
        + sem_pair(n_dp // 2 - 1)
        + sem_pair(n_f - 1)
        + sem_pair(n_dp - 1)
        + [pltpu.SemaphoreType.DMA((3 + 3 * GROUPS,))]
        + extra,
        compiler_params=pltpu.CompilerParams(
            vmem_limit_bytes=VMEM_LIMIT, collective_id=1, has_side_effects=True
        ),
        name="step",
    )(
        hidden_in,
        passage_lengths,
        query_lengths,
        partner,
        norm_gain,
        final_gain,
        queries.reshape(qrows, CDIM),
        *weights,
    )
    grad_input, grad_out, grad_head, losses = pl.pallas_call(
        finish_kernel,
        out_shape=(
            shape((tok, D), BF16),
            shape((shard, D), F32),
            shape((shard, CDIM), F32),
            shape((count,), F32),
        ),
        in_specs=[VM] * 4,
        out_specs=(HB, HB, HB, SM),
        scratch_shapes=[pltpu.SemaphoreType.DMA((3,))],
        compiler_params=pltpu.CompilerParams(vmem_limit_bytes=4 << 20),
        name="finish",
    )(*[pltpu.with_memory_space_constraint(a, pltpu.VMEM) for a in held])
    return losses, grad_input, grad_out, grad_head


def solution(mesh):
    placed = (
        P(("dp", "fsdp"), None),
        P(),
        P("fsdp", None),
        P("fsdp", None),
        P(),
        P("fsdp", None),
        P(("dp", "fsdp"), None, None),
        P(("dp", "fsdp")),
        P(("dp", "fsdp")),
        P(),
    )
    return jax.shard_map(
        functools.partial(per_device, mesh.shape["dp"], mesh.shape["fsdp"]),
        mesh=mesh,
        in_specs=placed,
        out_specs=(P(("dp", "fsdp")), P(("dp", "fsdp"), None), P("fsdp", None), P("fsdp", None)),
        check_vma=False,
    )
```

```python
import functools

import jax
import jax.numpy as jnp
from jax import lax
from jax.experimental import pallas as pl
from jax.experimental.pallas import tpu as pltpu
from jax.sharding import PartitionSpec as P

D = 768
HEADS = 12
HD = D // HEADS
CDIM = 128
WIN = 64
PLEN = 256
QLEN = 32
NB = 256
QB = 128
KB = QB + WIN
SPANS = PLEN // QB
UNROLL = 2
RB = 128

norm_eps = 1e-05
vec_eps = 1e-06
soft_temp = 0.05
masked_fill = -1e30

MESH = pl.DeviceIdType.MESH
F32 = jnp.float32
BF16 = jnp.bfloat16


def dot_nn(a, b):
    return lax.dot_general(a, b, (((1,), (0,)), ((), ())), preferred_element_type=F32)


def dot_nt(a, b):
    return lax.dot_general(a, b, (((1,), (1,)), ((), ())), preferred_element_type=F32)


def dot_tn(a, b):
    return lax.dot_general(a, b, (((0,), (0,)), ((), ())), preferred_element_type=F32)


def stats(rows):
    centered = rows - jnp.mean(rows, axis=-1, keepdims=True)
    inv_std = lax.rsqrt(jnp.mean(centered * centered, axis=-1, keepdims=True) + norm_eps)
    return centered * inv_std, inv_std


def row_loop(count, body):
    def step(i, carry):
        body(pl.ds(pl.multiple_of(i * RB, RB), RB))
        return carry

    lax.fori_loop(0, count // RB, step, 0)


def block_loop(count, body):
    def step(n, carry):
        body(n, pl.ds(pl.multiple_of(n * NB, NB), NB))
        return carry

    lax.fori_loop(0, count // NB, step, 0)


def fill_bias(len_ref, bias, passages):
    for b in range(SPANS):
        key = lax.broadcasted_iota(jnp.int32, (KB, QB), 0) + b * WIN
        query = lax.broadcasted_iota(jnp.int32, (KB, QB), 1) + b * QB
        in_band = jnp.abs(key - query) <= WIN
        for p in range(passages):
            allowed = in_band & ((key < len_ref[p]) | (key == query))
            bias[p * SPANS + b] = jnp.where(allowed, 0.0, masked_fill)


def half_masks():
    lane = lax.broadcasted_iota(jnp.int32, (QB, 128), 1)
    low = lane < HD
    keep = jnp.where(low, 1.0, 0.0)
    return low, (keep.astype(BF16), (1.0 - keep).astype(BF16))


def probs_of(scores):
    shifted = jnp.exp(scores - jnp.max(scores, axis=0, keepdims=True))
    return shifted * (1.0 / jnp.sum(shifted, axis=0, keepdims=True))


def greet(peers):
    barrier = pltpu.get_barrier_semaphore()
    for peer in peers:
        pl.semaphore_signal(barrier, inc=1, device_id=peer, device_id_type=MESH)
    return lambda: pl.semaphore_wait(barrier, len(peers))


def send(src, dst, sems, at, peer):
    copy = pltpu.make_async_remote_copy(
        src_ref=src,
        dst_ref=dst,
        send_sem=sems[0].at[at],
        recv_sem=sems[1].at[at],
        device_id=peer,
        device_id_type=MESH,
    )
    copy.start()
    return copy


GROUPS = 3
FIRST = 512
GW = D // GROUPS


def head_at(g, w):
    return pl.multiple_of(g * 3 * GW + w * 128, 128)


def step_kernel(
    n_dp,
    n_f,
    gathered,
    x_hbm,
    len_ref,
    qlen_ref,
    partner_ref,
    gain_ref,
    fgain_ref,
    quer_ref,
    qkvw_ref,
    outw_hbm,
    headw_hbm,
    gin_ref,
    gout_ref,
    ghead_ref,
    loss_ref,
    x_ref,
    w_ref,
    outw_ref,
    headw_ref,
    qkv_ref,
    ctx_ref,
    ctx_t,
    pack_ref,
    normed,
    x_norm,
    inv_x,
    mine,
    res,
    inv_res,
    pooled,
    emb,
    rgb,
    rg_ref,
    dctx_ref,
    wgrad_ref,
    grads,
    bias,
    saved,
    tile,
    got,
    stage_a,
    r0_a,
    pre_a,
    r1_a,
    acc_a,
    s2_a,
    r2_a,
    stage_b,
    r0_b,
    pre_b,
    r1_b,
    acc_b,
    s2_b,
    r2_b,
    s3,
    r3,
    *sems,
):
    q_sems, m_sems, c0_sems, c1_sems, h_sems, z_sems, zb_sems, hb_sems, g3_sems = [
        sems[2 * i : 2 * i + 2] for i in range(9)
    ]
    sems = sems[18:]
    l_sem = sems[0]
    rows_all = x_ref.shape[0]
    passages = rows_all // PLEN
    me = lax.axis_index("dp")
    my_f = lax.axis_index("fsdp")
    dp_peers = [{"dp": lax.rem(me + off, n_dp)} for off in range(1, n_dp)]
    f_peers = [{"fsdp": lax.rem(my_f + off, n_f)} for off in range(1, n_f)]
    ready = greet(dp_peers + f_peers)
    gain = gain_ref[...].reshape(1, D)
    fgain = fgain_ref[...].reshape(1, D)

    shard = gout_ref.shape[0]
    rows_in = qkvw_ref.shape[0]
    first_row = 0 if gathered else pl.multiple_of(my_f * shard, 16)
    own_rows = pl.ds(first_row, rows_in)
    x_copy = pltpu.make_async_copy(x_hbm, x_ref, l_sem.at[0])
    w_copies = []
    for g in range(GROUPS):
        for part in range(3):
            copy = pltpu.make_async_copy(
                qkvw_ref.at[:, pl.ds(part * D + g * GW, GW)],
                w_ref.at[own_rows, pl.ds((g * 3 + part) * GW, GW)],
                l_sem.at[3 + g * 3 + part],
            )
            copy.start()
            w_copies.append(copy)
    oh_copies = [
        pltpu.make_async_copy(outw_hbm, outw_ref.at[own_rows, :], l_sem.at[1]),
        pltpu.make_async_copy(headw_hbm, headw_ref.at[own_rows, :], l_sem.at[2]),
    ]
    x_copy.start()
    for copy in oh_copies:
        copy.start()

    q_count = quer_ref.shape[0]
    mine[0:q_count, :] = quer_ref[...]
    row = lax.broadcasted_iota(jnp.int32, (16, CDIM), 0)
    lens = jnp.zeros((16, CDIM), F32)
    for a in range(passages):
        lens = jnp.where(row == a, qlen_ref[a].astype(F32), lens)
    mine[q_count : q_count + 16, :] = lens.astype(BF16)
    ready()

    pending = []
    steps = GROUPS + 1
    a_all, b_all, c_all = [None] * steps, [None] * steps, [None] * steps
    if not gathered:
        a_sems, b_sems, c_sems = sems[1:3], sems[3:5], sems[5:7]
        halves = n_dp // 2
        part = shard // halves
        h, c = me // 2, lax.rem(me, 2)
        sibling = {"dp": 2 * h + 1 - c}

        def block(i, f, hh):
            ref, base = (w_ref, i * 3 * GW) if i < GROUPS else (outw_ref, 0)
            width = 3 * GW // 2
            rows = pl.ds(pl.multiple_of(f * shard + hh * part, 16), part)
            return ref.at[rows, pl.ds(pl.multiple_of(base + c * width, 128), width)]

        def start_a(i):
            copies = []
            for k in range(1, n_f):
                piece = headw_ref.at[own_rows, :] if i == steps else block(i, my_f, h)
                copies.append(send(piece, piece, a_sems, i * (n_f - 1) + k - 1, f_peers[k - 1]))
            pending.extend(copies)
            return copies

        def from_f(k):
            return lax.rem(my_f + n_f - k, n_f)

        def from_h(j):
            return lax.rem(h + halves - j, halves)

        def at_b(i, k, j):
            return (i * (n_f - 1) + k - 1) * halves + j

    def spread(i):
        if gathered:
            return
        b_copies, c_copies = [], []
        for k in range(1, n_f):
            a_all[i][k - 1].wait_recv()
            piece = block(i, from_f(k), h)
            for j in range(1, halves):
                peer = {"dp": 2 * lax.rem(h + j, halves) + c}
                b_copies.append((k, j, send(piece, piece, b_sems, at_b(i, k, j), peer)))
            c_copies.append(send(piece, piece, c_sems, at_b(i, k, 0), sibling))
        pending.extend([copy for _, _, copy in b_copies])
        b_all[i], c_all[i] = b_copies, c_copies

    def share(i):
        if gathered:
            return
        for k, j, copy in b_all[i]:
            copy.wait_recv()
            piece = block(i, from_f(k), from_h(j))
            c_all[i].append(send(piece, piece, c_sems, at_b(i, k, j), sibling))
        pending.extend(c_all[i])

    def arrive(i):
        if gathered:
            return
        for copy in c_all[i]:
            copy.wait_recv()

    for g in range(GROUPS):
        for copy in w_copies[3 * g : 3 * g + 3]:
            copy.wait()
        if not gathered:
            a_all[g] = start_a(g)
    for copy in oh_copies:
        copy.wait()
    if not gathered:
        a_all[GROUPS] = start_a(GROUPS)
    q_copies = [
        send(mine, pack_ref.at[me], q_sems, off, dp_peers[off]) for off in range(n_dp - 1)
    ]
    pending.extend(q_copies)
    pack_ref[me] = mine[...]
    x_copy.wait()
    spread(0)
    spread(1)

    def norm_rows_in(rows):
        n, inv = stats(x_ref[rows, :].astype(F32))
        x_norm[rows, :] = n
        inv_x[rows, :] = inv
        normed[rows, :] = (n * gain).astype(BF16)

    row_loop(rows_all, norm_rows_in)
    share(0)
    spread(2)
    if not gathered:
        a_head = start_a(steps)
    fill_bias(len_ref, bias, passages)
    low, keeps = half_masks()

    def sides(rows):
        return jnp.concatenate([rows * keeps[0], rows * keeps[1]], axis=0)

    def spans(p, b):
        queries = pl.ds(pl.multiple_of(p * PLEN + b * QB, QB), QB)
        keys = pl.ds(pl.multiple_of(p * PLEN + b * WIN, WIN), KB)
        return queries, keys

    def project(g):
        for part in range(3):
            cols = slice((g * 3 + part) * GW, (g * 3 + part + 1) * GW)
            rows = dot_nn(normed[...], w_ref[:, cols])
            if part == 0:
                rows = rows * HD**-0.5
            qkv_ref[:, cols] = rows.astype(BF16)

    def attend(g):
        def pair(it, carry):
            p, w = it // (GW // 128), lax.rem(it, GW // 128)
            at = head_at(g, w)
            out_at = pl.multiple_of(g * GW + w * 128, 128)
            slot = (p * (HEADS // 2) + g * (GW // 128) + w) * SPANS
            for b in range(SPANS):
                qrows, krows = spans(p, b)
                scores = dot_nt(
                    qkv_ref[krows, pl.ds(at + GW, 128)], sides(qkv_ref[qrows, pl.ds(at, 128)])
                )
                both = []
                for side in range(2):
                    lanes = slice(side * QB, (side + 1) * QB)
                    probs = probs_of(scores[:, lanes] + bias[p * SPANS + b])
                    saved[slot + b, :, lanes] = probs
                    both.append(probs.astype(BF16))
                out = dot_tn(jnp.concatenate(both, axis=1), qkv_ref[krows, pl.ds(at + 2 * GW, 128)])
                ctx_ref[qrows, pl.ds(out_at, 128)] = jnp.where(low, out[:QB], out[QB:]).astype(BF16)
            return carry

        lax.fori_loop(0, passages * (GW // 128), pair, 0, unroll=UNROLL)

    arrive(0)
    project(0)
    attend(0)
    share(1)
    spread(GROUPS)
    arrive(1)
    project(1)
    attend(1)
    share(2)
    arrive(2)
    project(2)
    attend(2)
    share(GROUPS)
    arrive(GROUPS)
    if not gathered:
        for copy in a_head:
            copy.wait_recv()
    for copy in q_copies:
        copy.wait_recv()

    def out_project(n, cols):
        res[:, cols] = x_ref[:, cols].astype(F32) + dot_nn(ctx_ref[...], outw_ref[:, cols])

    block_loop(D, out_project)

    def norm_rows(rows):
        n, inv = stats(res[rows, :])
        res[rows, :] = n
        inv_res[rows, :] = inv
        pooled[rows, :] = (n * fgain).astype(BF16)

    row_loop(rows_all, norm_rows)
    emb[...] = dot_nn(pooled[...], headw_ref[...])
    embedded = emb[...]
    inv_len = lax.rsqrt(jnp.sum(embedded * embedded, axis=-1, keepdims=True) + vec_eps)
    vectors = (embedded * inv_len).astype(BF16)
    q_near = passages * QLEN
    target = partner_ref[me]
    source = jnp.int32(0)
    for d in range(n_dp):
        source = jnp.where(partner_ref[d] == me, d, source)
    packs = (pack_ref[me], pack_ref[source])
    qf = jnp.concatenate([pack[:q_near].astype(F32) for pack in packs], axis=0)
    token = lax.broadcasted_iota(jnp.int32, (QLEN, CDIM), 0).astype(F32)
    masks = []
    for pack in packs:
        lens = pack[q_near : q_near + 16].astype(F32)
        for a in range(passages):
            masks.append(jnp.where(token < lens[a : a + 1], 1.0, 0.0))
    qmask = jnp.concatenate(masks, axis=0)[:, 0:1]
    qv = (qf * lax.rsqrt(jnp.sum(qf * qf, axis=-1, keepdims=True) + vec_eps)).astype(BF16)
    slot = lax.broadcasted_iota(jnp.int32, (1, PLEN), 1)
    live = jnp.concatenate(
        [jnp.where(slot < len_ref[b], 1.0, 0.0) for b in range(passages)], axis=1
    )
    weight = jnp.exp(dot_nt(qv, vectors) * (1.0 / soft_temp)) * live
    dens = [
        jnp.sum(weight[:, b * PLEN : (b + 1) * PLEN], axis=-1, keepdims=True)
        for b in range(passages)
    ]
    terms = [qmask * soft_temp * jnp.log(den) for den in dens]
    for q in range(2 * passages):
        for b in range(passages):
            total = jnp.sum(terms[b][q * QLEN : (q + 1) * QLEN], axis=0, keepdims=True)
            tile[q * passages + b : q * passages + b + 1, :] = jnp.broadcast_to(total, (1, 128))

    m_copies = [send(tile, got.at[me], m_sems, off, dp_peers[off]) for off in range(n_dp - 1)]
    got[me] = tile[...]

    def turn_context(n, cols):
        ctx_t[cols, :] = ctx_ref[:, cols].T

    block_loop(D, turn_context)
    for copy in m_copies:
        copy.wait()
    own = tile[...]
    from_target = got[target]
    from_source = got[source]
    half = passages * passages

    def logits_of(local, far, a):
        parts = [local[a * passages + b : a * passages + b + 1] for b in range(passages)]
        parts += [
            far[half + a * passages + b : half + a * passages + b + 1] for b in range(passages)
        ]
        total = jnp.exp(parts[0])
        for part in parts[1:]:
            total = total + jnp.exp(part)
        return parts, jnp.log(total)

    coef = [[] for _ in range(passages)]
    loss_ref[...] = jnp.zeros_like(loss_ref)
    for a in range(passages):
        parts, log_total = logits_of(own, from_target, a)
        loss_ref[a : a + 1, :] = log_total - parts[a]
        for b in range(passages):
            grad = jnp.exp(parts[b] - log_total) - (1.0 if a == b else 0.0)
            coef[b].append(jnp.broadcast_to(grad, (QLEN, 128)))
    for a in range(passages):
        parts, log_total = logits_of(from_source, own, a)
        for b in range(passages):
            grad = jnp.exp(parts[passages + b] - log_total)
            coef[b].append(jnp.broadcast_to(grad, (QLEN, 128)))
    for b in range(passages):
        rows = slice(b * PLEN, (b + 1) * PLEN)
        factor = jnp.concatenate(coef[b], axis=0)[:, 0:1] * qmask / dens[b]
        sim_grad = (weight[:, rows] * factor).astype(BF16)
        near = dot_tn(sim_grad[:q_near], qv[:q_near])
        far = dot_tn(sim_grad[q_near:], qv[q_near:]).astype(BF16).astype(F32)
        vgrad = near + far
        e, il = embedded[rows], inv_len[rows]
        along = jnp.sum(e * vgrad, axis=-1, keepdims=True)
        emb[rows, :] = il * vgrad - e * (il * il * il) * along
    emb_grad = emb[...].astype(BF16)
    wgrad_ref[:, D:] = dot_tn(pooled[...], emb_grad)

    def pool_back(n, cols):
        rg_ref[:, cols] = dot_nt(emb_grad, headw_ref[cols, :])

    block_loop(D, pool_back)

    def norm_back(rows):
        s = rg_ref[rows, :] * fgain
        n = res[rows, :]
        grad = inv_res[rows, :] * (
            s
            - jnp.mean(s, axis=-1, keepdims=True)
            - n * jnp.mean(s * n, axis=-1, keepdims=True)
        )
        rg_ref[rows, :] = grad
        rgb[rows, :] = grad.astype(BF16)

    row_loop(rows_all, norm_back)

    def out_back(n, cols):
        wgrad_ref[cols, :D] = dot_nn(ctx_t[cols, :], rgb[...])

    block_loop(D, out_back)

    thin = s3.shape[0]
    used = shard // thin
    quads = n_dp // 2
    my_h, my_c = me // 2, lax.rem(me, 2)
    pair = {"dp": 2 * my_h + 1 - my_c}
    near_quads = [lax.rem(my_h + off, quads) for off in range(1, quads)]
    near_rows = [lax.rem(my_f + off, n_f) for off in range(1, n_f)]

    def to_pair(stage, r0, sems, cols):
        for d in range(n_dp):
            for f in range(n_f):
                if d < used:
                    piece = wgrad_ref[f * shard + d * thin : f * shard + (d + 1) * thin, cols]
                    stage[d, f] = piece.astype(BF16)
                else:
                    stage[d, f] = jnp.zeros(stage.shape[2:], BF16)
        return [
            send(stage.at[2 * hh + 1 - my_c], r0.at[hh], sems, hh, pair) for hh in range(quads)
        ]

    def to_quads(src, dst, sems):
        return [
            send(src.at[hh], dst.at[my_h], sems, i, {"dp": 2 * hh + my_c})
            for i, hh in enumerate(near_quads)
        ]

    def to_rows(src, dst, sems):
        return [
            send(src.at[f], dst.at[my_f], sems, i, f_peers[i]) for i, f in enumerate(near_rows)
        ]

    def landed(copies):
        for copy in copies:
            copy.wait_recv()

    g0_a = to_pair(stage_a, r0_a, c0_sems, slice(0, FIRST))
    g0_b = to_pair(stage_b, r0_b, c1_sems, slice(FIRST, D + CDIM))

    def context_back(n, cols):
        dctx_ref[:, cols] = dot_nt(rgb[...], outw_ref[cols, :]).astype(BF16)

    block_loop(D, context_back)

    pairs = HEADS // 2

    def heads(first, last):
        def pair(it, carry):
            p, hp = it // pairs, lax.rem(it, pairs)
            at = head_at(hp // (GW // 128), lax.rem(hp, GW // 128))
            d_at = pl.multiple_of(hp * 128, 128)
            kg, vg = [], []
            for b in range(SPANS):
                qrows, krows = spans(p, b)
                q2 = sides(qkv_ref[qrows, pl.ds(at, 128)])
                d2 = sides(dctx_ref[qrows, pl.ds(d_at, 128)])
                k2 = qkv_ref[krows, pl.ds(at + GW, 128)]
                prob_grad = dot_nt(qkv_ref[krows, pl.ds(at + 2 * GW, 128)], d2)
                probs_b, score_b = [], []
                for side in range(2):
                    lanes = slice(side * QB, (side + 1) * QB)
                    probs, grad = saved[it * SPANS + b, :, lanes], prob_grad[:, lanes]
                    inner = jnp.sum(probs * grad, axis=0, keepdims=True)
                    probs_b.append(probs.astype(BF16))
                    score_b.append((probs * (grad - inner)).astype(BF16))
                score_grad = jnp.concatenate(score_b, axis=1)
                vg.append(dot_nn(jnp.concatenate(probs_b, axis=1), d2))
                kg.append(dot_nn(score_grad, q2))
                qg = dot_tn(score_grad, k2)
                qg = jnp.where(low, qg[:QB], qg[QB:]) * HD**-0.5
                grads[qrows, pl.ds(at, 128)] = qg.astype(BF16)
            rows = pl.ds(pl.multiple_of(p * PLEN, PLEN), PLEN)
            for offset, parts in ((GW, kg), (2 * GW, vg)):
                lower, upper = parts
                whole = jnp.concatenate(
                    [lower[:WIN], lower[WIN:] + upper[: KB - WIN], upper[KB - WIN :]], axis=0
                )
                grads[rows, pl.ds(at + offset, 128)] = whole.astype(BF16)
            return carry

        lax.fori_loop(first, last, pair, 0, unroll=UNROLL)

    heads(0, 2)
    landed(g0_a)
    for hh in range(quads):
        for f in range(n_f):
            both = stage_a[2 * hh + my_c, f].astype(F32) + r0_a[hh, f].astype(F32)
            pre_a[hh, f] = both.astype(BF16)
    g1_a = to_quads(pre_a, r1_a, h_sems)
    landed(g0_b)
    for f in range(n_f):
        for hh in range(quads):
            both = stage_b[2 * hh + my_c, f].astype(F32) + r0_b[hh, f].astype(F32)
            pre_b[f, hh] = both.astype(BF16)
    g1_b = to_rows(pre_b, r1_b, zb_sems)
    heads(2, passages * pairs)
    landed(g1_a)
    for f in range(n_f):
        total = pre_a[my_h, f].astype(F32)
        for hh in near_quads:
            total = total + r1_a[hh, f].astype(F32)
        acc_a[f] = total
        s2_a[f] = total.astype(BF16)
    g2_a = to_rows(s2_a, r2_a, z_sems)
    landed(g1_b)
    for hh in range(quads):
        total = pre_b[my_f, hh].astype(F32)
        for f in near_rows:
            total = total + r1_b[f, hh].astype(F32)
        acc_b[hh] = total
        s2_b[hh] = total.astype(BF16)
    g2_b = to_quads(s2_b, r2_b, hb_sems)

    def project_back(n, cols):
        res[:, cols] = dot_nt(grads[...], w_ref[cols, :])

    block_loop(D, project_back)
    landed(g2_a)
    total = acc_a[my_f]
    for f in near_rows:
        total = total + r2_a[f].astype(F32)
    s3[:, :FIRST] = total.astype(BF16)
    landed(g2_b)
    total = acc_b[my_h]
    for hh in near_quads:
        total = total + r2_b[hh].astype(F32)
    s3[:, FIRST:] = total.astype(BF16)
    g3 = [send(s3, r3.at[me], g3_sems, off, dp_peers[off]) for off in range(n_dp - 1)]
    r3[me] = s3[...]

    def norm_back_in(rows):
        n = x_norm[rows, :]
        t = res[rows, :] * gain
        grad = inv_x[rows, :] * (
            t
            - jnp.mean(t, axis=-1, keepdims=True)
            - n * jnp.mean(t * n, axis=-1, keepdims=True)
        )
        gin_ref[rows, :] = (rg_ref[rows, :] + grad).astype(BF16)

    row_loop(rows_all, norm_back_in)
    for copy in g3:
        copy.wait_recv()
    for d in range(used):
        piece = r3[d].astype(F32)
        gout_ref[d * thin : (d + 1) * thin, :] = piece[:, :D]
        ghead_ref[d * thin : (d + 1) * thin, :] = piece[:, D:]
    for copy in pending + g0_a + g0_b + g1_a + g1_b + g2_a + g2_b + g3:
        copy.wait_send()


def finish_kernel(gin, gout, ghead, loss, gin_out, gout_out, ghead_out, loss_out, sems):
    copies = [
        pltpu.make_async_copy(source, target, sems.at[i])
        for i, (source, target) in enumerate(
            ((gin, gin_out), (gout, gout_out), (ghead, ghead_out))
        )
    ]
    for copy in copies:
        copy.start()
    for a in range(loss_out.shape[0]):
        loss_out[a] = jnp.max(loss[a : a + 1, :])
    for copy in copies:
        copy.wait()


VM = pl.BlockSpec(memory_space=pltpu.VMEM)
SM = pl.BlockSpec(memory_space=pltpu.SMEM)
HB = pl.BlockSpec(memory_space=pl.ANY)
VMEM_LIMIT = 56 << 20


def sem_pair(count):
    return [pltpu.SemaphoreType.DMA((count,))] * 2


def per_device(
    n_dp,
    n_f,
    hidden_in,
    norm_gain,
    qkv_weight,
    out_weight,
    final_gain,
    head_weight,
    queries,
    query_lengths,
    passage_lengths,
    partner,
):
    tok = hidden_in.shape[0]
    count = passage_lengths.shape[0]
    qrows = count * QLEN
    shape = jax.ShapeDtypeStruct
    shard = qkv_weight.shape[0]
    weights = (qkv_weight, out_weight, head_weight)
    gathered = n_dp % 2 != 0 or shard % (8 * n_dp) != 0
    if gathered:
        weights = tuple(lax.all_gather(w, "fsdp", axis=0, tiled=True) for w in weights)
    copies = (n_f - 1) * n_dp // 2
    steps = GROUPS + 1
    extra = (
        []
        if gathered
        else sem_pair((steps + 1) * (n_f - 1))
        + sem_pair(steps * copies)
        + sem_pair(steps * copies)
    )
    thin = -(-shard // (8 * n_dp)) * 8
    wide = D + CDIM
    held = pl.pallas_call(
        functools.partial(step_kernel, n_dp, n_f, gathered),
        out_shape=(
            pltpu.VMEM((tok, D), BF16),
            pltpu.VMEM((shard, D), F32),
            pltpu.VMEM((shard, CDIM), F32),
            pltpu.VMEM((8, 128), F32),
        ),
        in_specs=[HB, SM, SM, SM, VM, VM, VM, HB, HB, HB],
        out_specs=(VM,) * 4,
        scratch_shapes=[
            pltpu.VMEM((tok, D), BF16),
            pltpu.VMEM((D, 3 * D), BF16),
            pltpu.VMEM((D, D), BF16),
            pltpu.VMEM((D, CDIM), BF16),
            pltpu.VMEM((tok, 3 * D), BF16),
            pltpu.VMEM((tok, D), BF16),
            pltpu.VMEM((D, tok), BF16),
            pltpu.VMEM((n_dp, qrows + 16, CDIM), BF16),
            pltpu.VMEM((tok, D), BF16),
            pltpu.VMEM((tok, D), F32),
            pltpu.VMEM((tok, 1), F32),
            pltpu.VMEM((qrows + 16, CDIM), BF16),
            pltpu.VMEM((tok, D), F32),
            pltpu.VMEM((tok, 1), F32),
            pltpu.VMEM((tok, D), BF16),
            pltpu.VMEM((tok, CDIM), F32),
            pltpu.VMEM((tok, D), BF16),
            pltpu.VMEM((tok, D), F32),
            pltpu.VMEM((tok, D), BF16),
            pltpu.VMEM((D, wide), F32),
            pltpu.VMEM((tok, 3 * D), BF16),
            pltpu.VMEM((count * SPANS, KB, QB), F32),
            pltpu.VMEM((count * (HEADS // 2) * SPANS, KB, 2 * QB), F32),
            pltpu.VMEM((2 * count * count, 128), F32),
            pltpu.VMEM((n_dp, 2 * count * count, 128), F32),
            pltpu.VMEM((n_dp, n_f, thin, FIRST), BF16),
            pltpu.VMEM((n_dp // 2, n_f, thin, FIRST), BF16),
            pltpu.VMEM((n_dp // 2, n_f, thin, FIRST), BF16),
            pltpu.VMEM((n_dp // 2, n_f, thin, FIRST), BF16),
            pltpu.VMEM((n_f, thin, FIRST), F32),
            pltpu.VMEM((n_f, thin, FIRST), BF16),
            pltpu.VMEM((n_f, thin, FIRST), BF16),
            pltpu.VMEM((n_dp, n_f, thin, wide - FIRST), BF16),
            pltpu.VMEM((n_dp // 2, n_f, thin, wide - FIRST), BF16),
            pltpu.VMEM((n_f, n_dp // 2, thin, wide - FIRST), BF16),
            pltpu.VMEM((n_f, n_dp // 2, thin, wide - FIRST), BF16),
            pltpu.VMEM((n_dp // 2, thin, wide - FIRST), F32),
            pltpu.VMEM((n_dp // 2, thin, wide - FIRST), BF16),
            pltpu.VMEM((n_dp // 2, thin, wide - FIRST), BF16),
            pltpu.VMEM((thin, wide), BF16),
            pltpu.VMEM((n_dp, thin, wide), BF16),
        ]
        + sem_pair(n_dp - 1)
        + sem_pair(n_dp - 1)
        + sem_pair(n_dp // 2)
        + sem_pair(n_dp // 2)
        + sem_pair(n_dp // 2 - 1)
        + sem_pair(n_f - 1)
        + sem_pair(n_f - 1)
        + sem_pair(n_dp // 2 - 1)
        + sem_pair(n_dp - 1)
        + [pltpu.SemaphoreType.DMA((3 + 3 * GROUPS,))]
        + extra,
        compiler_params=pltpu.CompilerParams(
            vmem_limit_bytes=VMEM_LIMIT, collective_id=1, has_side_effects=True
        ),
        name="step",
    )(
        hidden_in,
        passage_lengths,
        query_lengths,
        partner,
        norm_gain,
        final_gain,
        queries.reshape(qrows, CDIM),
        *weights,
    )
    grad_input, grad_out, grad_head, losses = pl.pallas_call(
        finish_kernel,
        out_shape=(
            shape((tok, D), BF16),
            shape((shard, D), F32),
            shape((shard, CDIM), F32),
            shape((count,), F32),
        ),
        in_specs=[VM] * 4,
        out_specs=(HB, HB, HB, SM),
        scratch_shapes=[pltpu.SemaphoreType.DMA((3,))],
        compiler_params=pltpu.CompilerParams(vmem_limit_bytes=4 << 20),
        name="finish",
    )(*[pltpu.with_memory_space_constraint(a, pltpu.VMEM) for a in held])
    return losses, grad_input, grad_out, grad_head


def solution(mesh):
    placed = (
        P(("dp", "fsdp"), None),
        P(),
        P("fsdp", None),
        P("fsdp", None),
        P(),
        P("fsdp", None),
        P(("dp", "fsdp"), None, None),
        P(("dp", "fsdp")),
        P(("dp", "fsdp")),
        P(),
    )
    return jax.shard_map(
        functools.partial(per_device, mesh.shape["dp"], mesh.shape["fsdp"]),
        mesh=mesh,
        in_specs=placed,
        out_specs=(P(("dp", "fsdp")), P(("dp", "fsdp"), None), P("fsdp", None), P("fsdp", None)),
        check_vma=False,
    )
```

```python
import functools

import jax
import jax.numpy as jnp
from jax import lax
from jax.experimental import pallas as pl
from jax.experimental.pallas import tpu as pltpu
from jax.sharding import PartitionSpec as P

D = 768
HEADS = 12
HD = D // HEADS
CDIM = 128
WIN = 64
PLEN = 256
QLEN = 32
NB = 256
QB = 128
KB = QB + WIN
SPANS = PLEN // QB
UNROLL = 2
RB = 128

norm_eps = 1e-05
vec_eps = 1e-06
soft_temp = 0.05
masked_fill = -1e30

MESH = pl.DeviceIdType.MESH
F32 = jnp.float32
BF16 = jnp.bfloat16


def dot_nn(a, b):
    return lax.dot_general(a, b, (((1,), (0,)), ((), ())), preferred_element_type=F32)


def dot_nt(a, b):
    return lax.dot_general(a, b, (((1,), (1,)), ((), ())), preferred_element_type=F32)


def dot_tn(a, b):
    return lax.dot_general(a, b, (((0,), (0,)), ((), ())), preferred_element_type=F32)


def stats(rows):
    centered = rows - jnp.mean(rows, axis=-1, keepdims=True)
    inv_std = lax.rsqrt(jnp.mean(centered * centered, axis=-1, keepdims=True) + norm_eps)
    return centered * inv_std, inv_std


def row_loop(count, body):
    def step(i, carry):
        body(pl.ds(pl.multiple_of(i * RB, RB), RB))
        return carry

    lax.fori_loop(0, count // RB, step, 0)


def block_loop(count, body):
    def step(n, carry):
        body(n, pl.ds(pl.multiple_of(n * NB, NB), NB))
        return carry

    lax.fori_loop(0, count // NB, step, 0)


def fill_bias(len_ref, bias, passages):
    for b in range(SPANS):
        key = lax.broadcasted_iota(jnp.int32, (KB, QB), 0) + b * WIN
        query = lax.broadcasted_iota(jnp.int32, (KB, QB), 1) + b * QB
        in_band = jnp.abs(key - query) <= WIN
        for p in range(passages):
            allowed = in_band & ((key < len_ref[p]) | (key == query))
            bias[p * SPANS + b] = jnp.where(allowed, 0.0, masked_fill)


def half_masks():
    lane = lax.broadcasted_iota(jnp.int32, (QB, 128), 1)
    low = lane < HD
    keep = jnp.where(low, 1.0, 0.0)
    return low, (keep.astype(BF16), (1.0 - keep).astype(BF16))


def probs_of(scores):
    shifted = jnp.exp(scores - jnp.max(scores, axis=0, keepdims=True))
    return shifted * (1.0 / jnp.sum(shifted, axis=0, keepdims=True))


def greet(peers):
    barrier = pltpu.get_barrier_semaphore()
    for peer in peers:
        pl.semaphore_signal(barrier, inc=1, device_id=peer, device_id_type=MESH)
    return lambda: pl.semaphore_wait(barrier, len(peers))


def send(src, dst, sems, at, peer):
    copy = pltpu.make_async_remote_copy(
        src_ref=src,
        dst_ref=dst,
        send_sem=sems[0].at[at],
        recv_sem=sems[1].at[at],
        device_id=peer,
        device_id_type=MESH,
    )
    copy.start()
    return copy


GROUPS = 3
FIRST = 512
GW = D // GROUPS


def head_at(g, w):
    return pl.multiple_of(g * 3 * GW + w * 128, 128)


def step_kernel(
    n_dp,
    n_f,
    gathered,
    x_hbm,
    len_ref,
    qlen_ref,
    partner_ref,
    gain_ref,
    fgain_ref,
    quer_ref,
    qkvw_ref,
    outw_hbm,
    headw_hbm,
    gin_ref,
    gout_ref,
    ghead_ref,
    loss_ref,
    x_ref,
    w_ref,
    outw_ref,
    headw_ref,
    qkv_ref,
    ctx_ref,
    ctx_t,
    pack_ref,
    normed,
    x_norm,
    inv_x,
    mine,
    res,
    inv_res,
    pooled,
    emb,
    rgb,
    rg_ref,
    dctx_ref,
    wgrad_ref,
    grads,
    bias,
    saved,
    tile,
    got,
    stage_a,
    r0_a,
    pre_a,
    r1_a,
    acc_a,
    s2_a,
    r2_a,
    stage_b,
    r0_b,
    pre_b,
    r1_b,
    acc_b,
    s2_b,
    r2_b,
    s3,
    r3,
    *sems,
):
    q_sems, m_sems, c0_sems, c1_sems, h_sems, z_sems, zb_sems, hb_sems, g3_sems = [
        sems[2 * i : 2 * i + 2] for i in range(9)
    ]
    sems = sems[18:]
    l_sem = sems[0]
    rows_all = x_ref.shape[0]
    passages = rows_all // PLEN
    me = lax.axis_index("dp")
    my_f = lax.axis_index("fsdp")
    dp_peers = [{"dp": lax.rem(me + off, n_dp)} for off in range(1, n_dp)]
    f_peers = [{"fsdp": lax.rem(my_f + off, n_f)} for off in range(1, n_f)]
    ready = greet(dp_peers + f_peers)
    gain = gain_ref[...].reshape(1, D)
    fgain = fgain_ref[...].reshape(1, D)

    shard = gout_ref.shape[0]
    rows_in = qkvw_ref.shape[0]
    first_row = 0 if gathered else pl.multiple_of(my_f * shard, 16)
    own_rows = pl.ds(first_row, rows_in)
    x_copy = pltpu.make_async_copy(x_hbm, x_ref, l_sem.at[0])
    w_copies = []
    for g in range(GROUPS):
        for part in range(3):
            copy = pltpu.make_async_copy(
                qkvw_ref.at[:, pl.ds(part * D + g * GW, GW)],
                w_ref.at[own_rows, pl.ds((g * 3 + part) * GW, GW)],
                l_sem.at[3 + g * 3 + part],
            )
            copy.start()
            w_copies.append(copy)
    oh_copies = [
        pltpu.make_async_copy(outw_hbm, outw_ref.at[own_rows, :], l_sem.at[1]),
        pltpu.make_async_copy(headw_hbm, headw_ref.at[own_rows, :], l_sem.at[2]),
    ]
    x_copy.start()
    for copy in oh_copies:
        copy.start()

    q_count = quer_ref.shape[0]
    mine[0:q_count, :] = quer_ref[...]
    row = lax.broadcasted_iota(jnp.int32, (16, CDIM), 0)
    lens = jnp.zeros((16, CDIM), F32)
    for a in range(passages):
        lens = jnp.where(row == a, qlen_ref[a].astype(F32), lens)
    mine[q_count : q_count + 16, :] = lens.astype(BF16)
    ready()

    pending = []
    steps = GROUPS + 1
    a_all, b_all, c_all = [None] * steps, [None] * steps, [None] * steps
    if not gathered:
        a_sems, b_sems, c_sems = sems[1:3], sems[3:5], sems[5:7]
        halves = n_dp // 2
        part = shard // halves
        h, c = me // 2, lax.rem(me, 2)
        sibling = {"dp": 2 * h + 1 - c}

        def block(i, f, hh):
            ref, base = (w_ref, i * 3 * GW) if i < GROUPS else (outw_ref, 0)
            width = 3 * GW // 2
            rows = pl.ds(pl.multiple_of(f * shard + hh * part, 16), part)
            return ref.at[rows, pl.ds(pl.multiple_of(base + c * width, 128), width)]

        def start_a(i):
            copies = []
            for k in range(1, n_f):
                piece = headw_ref.at[own_rows, :] if i == steps else block(i, my_f, h)
                copies.append(send(piece, piece, a_sems, i * (n_f - 1) + k - 1, f_peers[k - 1]))
            pending.extend(copies)
            return copies

        def from_f(k):
            return lax.rem(my_f + n_f - k, n_f)

        def from_h(j):
            return lax.rem(h + halves - j, halves)

        def at_b(i, k, j):
            return (i * (n_f - 1) + k - 1) * halves + j

    def spread(i):
        if gathered:
            return
        b_copies, c_copies = [], []
        for k in range(1, n_f):
            a_all[i][k - 1].wait_recv()
            piece = block(i, from_f(k), h)
            for j in range(1, halves):
                peer = {"dp": 2 * lax.rem(h + j, halves) + c}
                b_copies.append((k, j, send(piece, piece, b_sems, at_b(i, k, j), peer)))
            c_copies.append(send(piece, piece, c_sems, at_b(i, k, 0), sibling))
        pending.extend([copy for _, _, copy in b_copies])
        b_all[i], c_all[i] = b_copies, c_copies

    def share(i):
        if gathered:
            return
        for k, j, copy in b_all[i]:
            copy.wait_recv()
            piece = block(i, from_f(k), from_h(j))
            c_all[i].append(send(piece, piece, c_sems, at_b(i, k, j), sibling))
        pending.extend(c_all[i])

    def arrive(i):
        if gathered:
            return
        for copy in c_all[i]:
            copy.wait_recv()

    for g in range(GROUPS):
        for copy in w_copies[3 * g : 3 * g + 3]:
            copy.wait()
        if not gathered:
            a_all[g] = start_a(g)
    for copy in oh_copies:
        copy.wait()
    if not gathered:
        a_all[GROUPS] = start_a(GROUPS)
    q_copies = [
        send(mine, pack_ref.at[me], q_sems, off, dp_peers[off]) for off in range(n_dp - 1)
    ]
    pending.extend(q_copies)
    pack_ref[me] = mine[...]
    x_copy.wait()
    spread(0)
    spread(1)

    def norm_rows_in(rows):
        n, inv = stats(x_ref[rows, :].astype(F32))
        x_norm[rows, :] = n
        inv_x[rows, :] = inv
        normed[rows, :] = (n * gain).astype(BF16)

    row_loop(rows_all, norm_rows_in)
    share(0)
    spread(2)
    if not gathered:
        a_head = start_a(steps)
    fill_bias(len_ref, bias, passages)
    low, keeps = half_masks()

    def sides(rows):
        return jnp.concatenate([rows * keeps[0], rows * keeps[1]], axis=0)

    def spans(p, b):
        queries = pl.ds(pl.multiple_of(p * PLEN + b * QB, QB), QB)
        keys = pl.ds(pl.multiple_of(p * PLEN + b * WIN, WIN), KB)
        return queries, keys

    def project(g):
        for part in range(3):
            cols = slice((g * 3 + part) * GW, (g * 3 + part + 1) * GW)
            rows = dot_nn(normed[...], w_ref[:, cols])
            if part == 0:
                rows = rows * HD**-0.5
            qkv_ref[:, cols] = rows.astype(BF16)

    def attend(g):
        def pair(it, carry):
            p, w = it // (GW // 128), lax.rem(it, GW // 128)
            at = head_at(g, w)
            out_at = pl.multiple_of(g * GW + w * 128, 128)
            slot = (p * (HEADS // 2) + g * (GW // 128) + w) * SPANS
            for b in range(SPANS):
                qrows, krows = spans(p, b)
                scores = dot_nt(
                    qkv_ref[krows, pl.ds(at + GW, 128)], sides(qkv_ref[qrows, pl.ds(at, 128)])
                )
                both = []
                for side in range(2):
                    lanes = slice(side * QB, (side + 1) * QB)
                    probs = probs_of(scores[:, lanes] + bias[p * SPANS + b])
                    saved[slot + b, :, lanes] = probs
                    both.append(probs.astype(BF16))
                out = dot_tn(jnp.concatenate(both, axis=1), qkv_ref[krows, pl.ds(at + 2 * GW, 128)])
                ctx_ref[qrows, pl.ds(out_at, 128)] = jnp.where(low, out[:QB], out[QB:]).astype(BF16)
            return carry

        lax.fori_loop(0, passages * (GW // 128), pair, 0, unroll=UNROLL)

    arrive(0)
    project(0)
    attend(0)
    share(1)
    spread(GROUPS)
    arrive(1)
    project(1)
    attend(1)
    share(2)
    arrive(2)
    project(2)
    attend(2)
    share(GROUPS)
    for copy in q_copies:
        copy.wait_recv()

    def out_project(n):
        half = lax.rem(lax.rem(me, 2) + n, 2)
        cols = pl.ds(pl.multiple_of(half * (D // 2), 128), D // 2)
        res[:, cols] = x_ref[:, cols].astype(F32) + dot_nn(ctx_ref[...], outw_ref[:, cols])

    out_project(0)
    arrive(GROUPS)
    out_project(1)
    if not gathered:
        for copy in a_head:
            copy.wait_recv()

    def norm_rows(rows):
        n, inv = stats(res[rows, :])
        res[rows, :] = n
        inv_res[rows, :] = inv
        pooled[rows, :] = (n * fgain).astype(BF16)

    row_loop(rows_all, norm_rows)
    emb[...] = dot_nn(pooled[...], headw_ref[...])
    embedded = emb[...]
    inv_len = lax.rsqrt(jnp.sum(embedded * embedded, axis=-1, keepdims=True) + vec_eps)
    vectors = (embedded * inv_len).astype(BF16)
    q_near = passages * QLEN
    target = partner_ref[me]
    source = jnp.int32(0)
    for d in range(n_dp):
        source = jnp.where(partner_ref[d] == me, d, source)
    packs = (pack_ref[me], pack_ref[source])
    qf = jnp.concatenate([pack[:q_near].astype(F32) for pack in packs], axis=0)
    token = lax.broadcasted_iota(jnp.int32, (QLEN, CDIM), 0).astype(F32)
    masks = []
    for pack in packs:
        lens = pack[q_near : q_near + 16].astype(F32)
        for a in range(passages):
            masks.append(jnp.where(token < lens[a : a + 1], 1.0, 0.0))
    qmask = jnp.concatenate(masks, axis=0)[:, 0:1]
    qv = (qf * lax.rsqrt(jnp.sum(qf * qf, axis=-1, keepdims=True) + vec_eps)).astype(BF16)
    slot = lax.broadcasted_iota(jnp.int32, (1, PLEN), 1)
    live = jnp.concatenate(
        [jnp.where(slot < len_ref[b], 1.0, 0.0) for b in range(passages)], axis=1
    )
    weight = jnp.exp(dot_nt(qv, vectors) * (1.0 / soft_temp)) * live
    dens = [
        jnp.sum(weight[:, b * PLEN : (b + 1) * PLEN], axis=-1, keepdims=True)
        for b in range(passages)
    ]
    terms = [qmask * soft_temp * jnp.log(den) for den in dens]
    for q in range(2 * passages):
        for b in range(passages):
            total = jnp.sum(terms[b][q * QLEN : (q + 1) * QLEN], axis=0, keepdims=True)
            tile[q * passages + b : q * passages + b + 1, :] = jnp.broadcast_to(total, (1, 128))

    m_copies = [send(tile, got.at[me], m_sems, off, dp_peers[off]) for off in range(n_dp - 1)]
    got[me] = tile[...]

    def turn_context(n, cols):
        ctx_t[cols, :] = ctx_ref[:, cols].T

    block_loop(D, turn_context)
    for copy in m_copies:
        copy.wait()
    own = tile[...]
    from_target = got[target]
    from_source = got[source]
    half = passages * passages

    def logits_of(local, far, a):
        parts = [local[a * passages + b : a * passages + b + 1] for b in range(passages)]
        parts += [
            far[half + a * passages + b : half + a * passages + b + 1] for b in range(passages)
        ]
        total = jnp.exp(parts[0])
        for part in parts[1:]:
            total = total + jnp.exp(part)
        return parts, jnp.log(total)

    coef = [[] for _ in range(passages)]
    loss_ref[...] = jnp.zeros_like(loss_ref)
    for a in range(passages):
        parts, log_total = logits_of(own, from_target, a)
        loss_ref[a : a + 1, :] = log_total - parts[a]
        for b in range(passages):
            grad = jnp.exp(parts[b] - log_total) - (1.0 if a == b else 0.0)
            coef[b].append(jnp.broadcast_to(grad, (QLEN, 128)))
    for a in range(passages):
        parts, log_total = logits_of(from_source, own, a)
        for b in range(passages):
            grad = jnp.exp(parts[passages + b] - log_total)
            coef[b].append(jnp.broadcast_to(grad, (QLEN, 128)))
    for b in range(passages):
        rows = slice(b * PLEN, (b + 1) * PLEN)
        factor = jnp.concatenate(coef[b], axis=0)[:, 0:1] * qmask / dens[b]
        sim_grad = (weight[:, rows] * factor).astype(BF16)
        near = dot_tn(sim_grad[:q_near], qv[:q_near])
        far = dot_tn(sim_grad[q_near:], qv[q_near:]).astype(BF16).astype(F32)
        vgrad = near + far
        e, il = embedded[rows], inv_len[rows]
        along = jnp.sum(e * vgrad, axis=-1, keepdims=True)
        emb[rows, :] = il * vgrad - e * (il * il * il) * along
    emb_grad = emb[...].astype(BF16)
    wgrad_ref[:, D:] = dot_tn(pooled[...], emb_grad)

    def pool_back(n, cols):
        rg_ref[:, cols] = dot_nt(emb_grad, headw_ref[cols, :])

    block_loop(D, pool_back)

    def norm_back(rows):
        s = rg_ref[rows, :] * fgain
        n = res[rows, :]
        grad = inv_res[rows, :] * (
            s
            - jnp.mean(s, axis=-1, keepdims=True)
            - n * jnp.mean(s * n, axis=-1, keepdims=True)
        )
        rg_ref[rows, :] = grad
        rgb[rows, :] = grad.astype(BF16)

    row_loop(rows_all, norm_back)

    def out_back(n, cols):
        wgrad_ref[cols, :D] = dot_nn(ctx_t[cols, :], rgb[...])

    block_loop(D, out_back)

    thin = s3.shape[0]
    used = shard // thin
    quads = n_dp // 2
    my_h, my_c = me // 2, lax.rem(me, 2)
    pair = {"dp": 2 * my_h + 1 - my_c}
    near_quads = [lax.rem(my_h + off, quads) for off in range(1, quads)]
    near_rows = [lax.rem(my_f + off, n_f) for off in range(1, n_f)]

    def to_pair(stage, r0, sems, cols):
        for d in range(n_dp):
            for f in range(n_f):
                if d < used:
                    piece = wgrad_ref[f * shard + d * thin : f * shard + (d + 1) * thin, cols]
                    stage[d, f] = piece.astype(BF16)
                else:
                    stage[d, f] = jnp.zeros(stage.shape[2:], BF16)
        return [
            send(stage.at[2 * hh + 1 - my_c], r0.at[hh], sems, hh, pair) for hh in range(quads)
        ]

    def to_quads(src, dst, sems):
        return [
            send(src.at[hh], dst.at[my_h], sems, i, {"dp": 2 * hh + my_c})
            for i, hh in enumerate(near_quads)
        ]

    def to_rows(src, dst, sems):
        return [
            send(src.at[f], dst.at[my_f], sems, i, f_peers[i]) for i, f in enumerate(near_rows)
        ]

    def landed(copies):
        for copy in copies:
            copy.wait_recv()

    g0_a = to_pair(stage_a, r0_a, c0_sems, slice(0, FIRST))
    g0_b = to_pair(stage_b, r0_b, c1_sems, slice(FIRST, D + CDIM))

    def context_back(n, cols):
        dctx_ref[:, cols] = dot_nt(rgb[...], outw_ref[cols, :]).astype(BF16)

    block_loop(D, context_back)

    pairs = HEADS // 2

    def heads(first, last):
        def pair(it, carry):
            p, hp = it // pairs, lax.rem(it, pairs)
            at = head_at(hp // (GW // 128), lax.rem(hp, GW // 128))
            d_at = pl.multiple_of(hp * 128, 128)
            kg, vg = [], []
            for b in range(SPANS):
                qrows, krows = spans(p, b)
                q2 = sides(qkv_ref[qrows, pl.ds(at, 128)])
                d2 = sides(dctx_ref[qrows, pl.ds(d_at, 128)])
                k2 = qkv_ref[krows, pl.ds(at + GW, 128)]
                prob_grad = dot_nt(qkv_ref[krows, pl.ds(at + 2 * GW, 128)], d2)
                probs_b, score_b = [], []
                for side in range(2):
                    lanes = slice(side * QB, (side + 1) * QB)
                    probs, grad = saved[it * SPANS + b, :, lanes], prob_grad[:, lanes]
                    inner = jnp.sum(probs * grad, axis=0, keepdims=True)
                    probs_b.append(probs.astype(BF16))
                    score_b.append((probs * (grad - inner)).astype(BF16))
                score_grad = jnp.concatenate(score_b, axis=1)
                vg.append(dot_nn(jnp.concatenate(probs_b, axis=1), d2))
                kg.append(dot_nn(score_grad, q2))
                qg = dot_tn(score_grad, k2)
                qg = jnp.where(low, qg[:QB], qg[QB:]) * HD**-0.5
                grads[qrows, pl.ds(at, 128)] = qg.astype(BF16)
            rows = pl.ds(pl.multiple_of(p * PLEN, PLEN), PLEN)
            for offset, parts in ((GW, kg), (2 * GW, vg)):
                lower, upper = parts
                whole = jnp.concatenate(
                    [lower[:WIN], lower[WIN:] + upper[: KB - WIN], upper[KB - WIN :]], axis=0
                )
                grads[rows, pl.ds(at + offset, 128)] = whole.astype(BF16)
            return carry

        lax.fori_loop(first, last, pair, 0, unroll=UNROLL)

    heads(0, 2)
    landed(g0_a)
    for hh in range(quads):
        for f in range(n_f):
            both = stage_a[2 * hh + my_c, f].astype(F32) + r0_a[hh, f].astype(F32)
            pre_a[hh, f] = both.astype(BF16)
    g1_a = to_quads(pre_a, r1_a, h_sems)
    landed(g0_b)
    for f in range(n_f):
        for hh in range(quads):
            both = stage_b[2 * hh + my_c, f].astype(F32) + r0_b[hh, f].astype(F32)
            pre_b[f, hh] = both.astype(BF16)
    g1_b = to_rows(pre_b, r1_b, zb_sems)
    heads(2, passages * pairs)
    landed(g1_a)
    for f in range(n_f):
        total = pre_a[my_h, f].astype(F32)
        for hh in near_quads:
            total = total + r1_a[hh, f].astype(F32)
        acc_a[f] = total
        s2_a[f] = total.astype(BF16)
    g2_a = to_rows(s2_a, r2_a, z_sems)
    landed(g1_b)
    for hh in range(quads):
        total = pre_b[my_f, hh].astype(F32)
        for f in near_rows:
            total = total + r1_b[f, hh].astype(F32)
        acc_b[hh] = total
        s2_b[hh] = total.astype(BF16)
    g2_b = to_quads(s2_b, r2_b, hb_sems)

    def project_back(n, cols):
        res[:, cols] = dot_nt(grads[...], w_ref[cols, :])

    block_loop(D, project_back)
    landed(g2_a)
    total = acc_a[my_f]
    for f in near_rows:
        total = total + r2_a[f].astype(F32)
    s3[:, :FIRST] = total.astype(BF16)
    landed(g2_b)
    total = acc_b[my_h]
    for hh in near_quads:
        total = total + r2_b[hh].astype(F32)
    s3[:, FIRST:] = total.astype(BF16)
    g3 = [send(s3, r3.at[me], g3_sems, off, dp_peers[off]) for off in range(n_dp - 1)]
    r3[me] = s3[...]

    def norm_back_in(rows):
        n = x_norm[rows, :]
        t = res[rows, :] * gain
        grad = inv_x[rows, :] * (
            t
            - jnp.mean(t, axis=-1, keepdims=True)
            - n * jnp.mean(t * n, axis=-1, keepdims=True)
        )
        gin_ref[rows, :] = (rg_ref[rows, :] + grad).astype(BF16)

    row_loop(rows_all, norm_back_in)
    for copy in g3:
        copy.wait_recv()
    for d in range(used):
        piece = r3[d].astype(F32)
        gout_ref[d * thin : (d + 1) * thin, :] = piece[:, :D]
        ghead_ref[d * thin : (d + 1) * thin, :] = piece[:, D:]
    for copy in pending + g0_a + g0_b + g1_a + g1_b + g2_a + g2_b + g3:
        copy.wait_send()


def finish_kernel(gin, gout, ghead, loss, gin_out, gout_out, ghead_out, loss_out, sems):
    copies = [
        pltpu.make_async_copy(source, target, sems.at[i])
        for i, (source, target) in enumerate(
            ((gin, gin_out), (gout, gout_out), (ghead, ghead_out))
        )
    ]
    for copy in copies:
        copy.start()
    for a in range(loss_out.shape[0]):
        loss_out[a] = jnp.max(loss[a : a + 1, :])
    for copy in copies:
        copy.wait()


VM = pl.BlockSpec(memory_space=pltpu.VMEM)
SM = pl.BlockSpec(memory_space=pltpu.SMEM)
HB = pl.BlockSpec(memory_space=pl.ANY)
VMEM_LIMIT = 56 << 20


def sem_pair(count):
    return [pltpu.SemaphoreType.DMA((count,))] * 2


def per_device(
    n_dp,
    n_f,
    hidden_in,
    norm_gain,
    qkv_weight,
    out_weight,
    final_gain,
    head_weight,
    queries,
    query_lengths,
    passage_lengths,
    partner,
):
    tok = hidden_in.shape[0]
    count = passage_lengths.shape[0]
    qrows = count * QLEN
    shape = jax.ShapeDtypeStruct
    shard = qkv_weight.shape[0]
    weights = (qkv_weight, out_weight, head_weight)
    gathered = n_dp % 2 != 0 or shard % (8 * n_dp) != 0
    if gathered:
        weights = tuple(lax.all_gather(w, "fsdp", axis=0, tiled=True) for w in weights)
    copies = (n_f - 1) * n_dp // 2
    steps = GROUPS + 1
    extra = (
        []
        if gathered
        else sem_pair((steps + 1) * (n_f - 1))
        + sem_pair(steps * copies)
        + sem_pair(steps * copies)
    )
    thin = -(-shard // (8 * n_dp)) * 8
    wide = D + CDIM
    held = pl.pallas_call(
        functools.partial(step_kernel, n_dp, n_f, gathered),
        out_shape=(
            pltpu.VMEM((tok, D), BF16),
            pltpu.VMEM((shard, D), F32),
            pltpu.VMEM((shard, CDIM), F32),
            pltpu.VMEM((8, 128), F32),
        ),
        in_specs=[HB, SM, SM, SM, VM, VM, VM, HB, HB, HB],
        out_specs=(VM,) * 4,
        scratch_shapes=[
            pltpu.VMEM((tok, D), BF16),
            pltpu.VMEM((D, 3 * D), BF16),
            pltpu.VMEM((D, D), BF16),
            pltpu.VMEM((D, CDIM), BF16),
            pltpu.VMEM((tok, 3 * D), BF16),
            pltpu.VMEM((tok, D), BF16),
            pltpu.VMEM((D, tok), BF16),
            pltpu.VMEM((n_dp, qrows + 16, CDIM), BF16),
            pltpu.VMEM((tok, D), BF16),
            pltpu.VMEM((tok, D), F32),
            pltpu.VMEM((tok, 1), F32),
            pltpu.VMEM((qrows + 16, CDIM), BF16),
            pltpu.VMEM((tok, D), F32),
            pltpu.VMEM((tok, 1), F32),
            pltpu.VMEM((tok, D), BF16),
            pltpu.VMEM((tok, CDIM), F32),
            pltpu.VMEM((tok, D), BF16),
            pltpu.VMEM((tok, D), F32),
            pltpu.VMEM((tok, D), BF16),
            pltpu.VMEM((D, wide), F32),
            pltpu.VMEM((tok, 3 * D), BF16),
            pltpu.VMEM((count * SPANS, KB, QB), F32),
            pltpu.VMEM((count * (HEADS // 2) * SPANS, KB, 2 * QB), F32),
            pltpu.VMEM((2 * count * count, 128), F32),
            pltpu.VMEM((n_dp, 2 * count * count, 128), F32),
            pltpu.VMEM((n_dp, n_f, thin, FIRST), BF16),
            pltpu.VMEM((n_dp // 2, n_f, thin, FIRST), BF16),
            pltpu.VMEM((n_dp // 2, n_f, thin, FIRST), BF16),
            pltpu.VMEM((n_dp // 2, n_f, thin, FIRST), BF16),
            pltpu.VMEM((n_f, thin, FIRST), F32),
            pltpu.VMEM((n_f, thin, FIRST), BF16),
            pltpu.VMEM((n_f, thin, FIRST), BF16),
            pltpu.VMEM((n_dp, n_f, thin, wide - FIRST), BF16),
            pltpu.VMEM((n_dp // 2, n_f, thin, wide - FIRST), BF16),
            pltpu.VMEM((n_f, n_dp // 2, thin, wide - FIRST), BF16),
            pltpu.VMEM((n_f, n_dp // 2, thin, wide - FIRST), BF16),
            pltpu.VMEM((n_dp // 2, thin, wide - FIRST), F32),
            pltpu.VMEM((n_dp // 2, thin, wide - FIRST), BF16),
            pltpu.VMEM((n_dp // 2, thin, wide - FIRST), BF16),
            pltpu.VMEM((thin, wide), BF16),
            pltpu.VMEM((n_dp, thin, wide), BF16),
        ]
        + sem_pair(n_dp - 1)
        + sem_pair(n_dp - 1)
        + sem_pair(n_dp // 2)
        + sem_pair(n_dp // 2)
        + sem_pair(n_dp // 2 - 1)
        + sem_pair(n_f - 1)
        + sem_pair(n_f - 1)
        + sem_pair(n_dp // 2 - 1)
        + sem_pair(n_dp - 1)
        + [pltpu.SemaphoreType.DMA((3 + 3 * GROUPS,))]
        + extra,
        compiler_params=pltpu.CompilerParams(
            vmem_limit_bytes=VMEM_LIMIT, collective_id=1, has_side_effects=True
        ),
        name="step",
    )(
        hidden_in,
        passage_lengths,
        query_lengths,
        partner,
        norm_gain,
        final_gain,
        queries.reshape(qrows, CDIM),
        *weights,
    )
    grad_input, grad_out, grad_head, losses = pl.pallas_call(
        finish_kernel,
        out_shape=(
            shape((tok, D), BF16),
            shape((shard, D), F32),
            shape((shard, CDIM), F32),
            shape((count,), F32),
        ),
        in_specs=[VM] * 4,
        out_specs=(HB, HB, HB, SM),
        scratch_shapes=[pltpu.SemaphoreType.DMA((3,))],
        compiler_params=pltpu.CompilerParams(vmem_limit_bytes=4 << 20),
        name="finish",
    )(*[pltpu.with_memory_space_constraint(a, pltpu.VMEM) for a in held])
    return losses, grad_input, grad_out, grad_head


def solution(mesh):
    placed = (
        P(("dp", "fsdp"), None),
        P(),
        P("fsdp", None),
        P("fsdp", None),
        P(),
        P("fsdp", None),
        P(("dp", "fsdp"), None, None),
        P(("dp", "fsdp")),
        P(("dp", "fsdp")),
        P(),
    )
    return jax.shard_map(
        functools.partial(per_device, mesh.shape["dp"], mesh.shape["fsdp"]),
        mesh=mesh,
        in_specs=placed,
        out_specs=(P(("dp", "fsdp")), P(("dp", "fsdp"), None), P("fsdp", None), P("fsdp", None)),
        check_vma=False,
    )
```

```python
import functools

import jax
import jax.numpy as jnp
from jax import lax
from jax.experimental import pallas as pl
from jax.experimental.pallas import tpu as pltpu
from jax.sharding import PartitionSpec as P

D = 768
HEADS = 12
HD = D // HEADS
CDIM = 128
WIN = 64
PLEN = 256
QLEN = 32
NB = 256
QB = 128
KB = QB + WIN
SPANS = PLEN // QB
UNROLL = 2
RB = 128

norm_eps = 1e-05
vec_eps = 1e-06
soft_temp = 0.05
masked_fill = -1e30

MESH = pl.DeviceIdType.MESH
F32 = jnp.float32
BF16 = jnp.bfloat16


def dot_nn(a, b):
    return lax.dot_general(a, b, (((1,), (0,)), ((), ())), preferred_element_type=F32)


def dot_nt(a, b):
    return lax.dot_general(a, b, (((1,), (1,)), ((), ())), preferred_element_type=F32)


def dot_tn(a, b):
    return lax.dot_general(a, b, (((0,), (0,)), ((), ())), preferred_element_type=F32)


def stats(rows):
    centered = rows - jnp.mean(rows, axis=-1, keepdims=True)
    inv_std = lax.rsqrt(jnp.mean(centered * centered, axis=-1, keepdims=True) + norm_eps)
    return centered * inv_std, inv_std


def row_loop(count, body):
    def step(i, carry):
        body(pl.ds(pl.multiple_of(i * RB, RB), RB))
        return carry

    lax.fori_loop(0, count // RB, step, 0)


def block_loop(count, body):
    def step(n, carry):
        body(n, pl.ds(pl.multiple_of(n * NB, NB), NB))
        return carry

    lax.fori_loop(0, count // NB, step, 0)


def fill_bias(len_ref, bias, passages):
    for b in range(SPANS):
        key = lax.broadcasted_iota(jnp.int32, (KB, QB), 0) + b * WIN
        query = lax.broadcasted_iota(jnp.int32, (KB, QB), 1) + b * QB
        in_band = jnp.abs(key - query) <= WIN
        for p in range(passages):
            allowed = in_band & ((key < len_ref[p]) | (key == query))
            bias[p * SPANS + b] = jnp.where(allowed, 0.0, masked_fill)


def half_masks():
    lane = lax.broadcasted_iota(jnp.int32, (QB, 128), 1)
    low = lane < HD
    keep = jnp.where(low, 1.0, 0.0)
    return low, (keep.astype(BF16), (1.0 - keep).astype(BF16))


def probs_of(scores):
    shifted = jnp.exp(scores - jnp.max(scores, axis=0, keepdims=True))
    return shifted * (1.0 / jnp.sum(shifted, axis=0, keepdims=True))


def greet(peers):
    barrier = pltpu.get_barrier_semaphore()
    for peer in peers:
        pl.semaphore_signal(barrier, inc=1, device_id=peer, device_id_type=MESH)
    return lambda: pl.semaphore_wait(barrier, len(peers))


def send(src, dst, sems, at, peer):
    copy = pltpu.make_async_remote_copy(
        src_ref=src,
        dst_ref=dst,
        send_sem=sems[0].at[at],
        recv_sem=sems[1].at[at],
        device_id=peer,
        device_id_type=MESH,
    )
    copy.start()
    return copy


GROUPS = 3
FIRST = 512
GW = D // GROUPS


def head_at(g, w):
    return pl.multiple_of(g * 3 * GW + w * 128, 128)


def step_kernel(
    n_dp,
    n_f,
    gathered,
    x_hbm,
    len_ref,
    qlen_ref,
    partner_ref,
    gain_ref,
    fgain_ref,
    quer_ref,
    qkvw_ref,
    outw_hbm,
    headw_hbm,
    gin_ref,
    gout_ref,
    ghead_ref,
    loss_ref,
    x_ref,
    w_ref,
    outw_ref,
    headw_ref,
    qkv_ref,
    ctx_ref,
    ctx_t,
    pack_ref,
    normed,
    x_norm,
    inv_x,
    mine,
    res,
    inv_res,
    pooled,
    emb,
    rgb,
    rg_ref,
    dctx_ref,
    wgrad_ref,
    grads,
    bias,
    saved,
    tile,
    got,
    stage_a,
    r0_a,
    pre_a,
    r1_a,
    acc_a,
    s2_a,
    r2_a,
    stage_b,
    r0_b,
    pre_b,
    r1_b,
    acc_b,
    s2_b,
    r2_b,
    s3,
    r3,
    *sems,
):
    q_sems, m_sems, c0_sems, c1_sems, h_sems, z_sems, zb_sems, hb_sems, g3_sems = [
        sems[2 * i : 2 * i + 2] for i in range(9)
    ]
    sems = sems[18:]
    l_sem = sems[0]
    rows_all = x_ref.shape[0]
    passages = rows_all // PLEN
    me = lax.axis_index("dp")
    my_f = lax.axis_index("fsdp")
    dp_peers = [{"dp": lax.rem(me + off, n_dp)} for off in range(1, n_dp)]
    f_peers = [{"fsdp": lax.rem(my_f + off, n_f)} for off in range(1, n_f)]
    ready = greet(dp_peers + f_peers)
    gain = gain_ref[...].reshape(1, D)
    fgain = fgain_ref[...].reshape(1, D)

    shard = gout_ref.shape[0]
    rows_in = qkvw_ref.shape[0]
    first_row = 0 if gathered else pl.multiple_of(my_f * shard, 16)
    own_rows = pl.ds(first_row, rows_in)
    x_copy = pltpu.make_async_copy(x_hbm, x_ref, l_sem.at[0])
    w_copies = []
    for g in range(GROUPS):
        for part in range(3):
            copy = pltpu.make_async_copy(
                qkvw_ref.at[:, pl.ds(part * D + g * GW, GW)],
                w_ref.at[own_rows, pl.ds((g * 3 + part) * GW, GW)],
                l_sem.at[3 + g * 3 + part],
            )
            copy.start()
            w_copies.append(copy)
    oh_copies = [
        pltpu.make_async_copy(outw_hbm, outw_ref.at[own_rows, :], l_sem.at[1]),
        pltpu.make_async_copy(headw_hbm, headw_ref.at[own_rows, :], l_sem.at[2]),
    ]
    x_copy.start()
    for copy in oh_copies:
        copy.start()

    q_count = quer_ref.shape[0]
    mine[0:q_count, :] = quer_ref[...]
    row = lax.broadcasted_iota(jnp.int32, (16, CDIM), 0)
    lens = jnp.zeros((16, CDIM), F32)
    for a in range(passages):
        lens = jnp.where(row == a, qlen_ref[a].astype(F32), lens)
    mine[q_count : q_count + 16, :] = lens.astype(BF16)
    ready()

    pending = []
    steps = GROUPS + 1
    a_all, b_all, c_all = [None] * steps, [None] * steps, [None] * steps
    if not gathered:
        a_sems, b_sems, c_sems = sems[1:3], sems[3:5], sems[5:7]
        halves = n_dp // 2
        part = shard // halves
        h, c = me // 2, lax.rem(me, 2)
        sibling = {"dp": 2 * h + 1 - c}

        def block(i, f, hh):
            ref, base = (w_ref, i * 3 * GW) if i < GROUPS else (outw_ref, 0)
            width = 3 * GW // 2
            rows = pl.ds(pl.multiple_of(f * shard + hh * part, 16), part)
            return ref.at[rows, pl.ds(pl.multiple_of(base + c * width, 128), width)]

        def head_half(f):
            half = shard // 2
            return headw_ref.at[pl.ds(pl.multiple_of(f * shard + c * half, 16), half), :]

        def start_a(i):
            copies = []
            for k in range(1, n_f):
                piece = head_half(my_f) if i == steps else block(i, my_f, h)
                copies.append(send(piece, piece, a_sems, i * (n_f - 1) + k - 1, f_peers[k - 1]))
            pending.extend(copies)
            return copies

        def from_f(k):
            return lax.rem(my_f + n_f - k, n_f)

        def from_h(j):
            return lax.rem(h + halves - j, halves)

        def at_b(i, k, j):
            return (i * (n_f - 1) + k - 1) * halves + j

    def spread(i):
        if gathered:
            return
        b_copies, c_copies = [], []
        for k in range(1, n_f):
            a_all[i][k - 1].wait_recv()
            piece = block(i, from_f(k), h)
            for j in range(1, halves):
                peer = {"dp": 2 * lax.rem(h + j, halves) + c}
                b_copies.append((k, j, send(piece, piece, b_sems, at_b(i, k, j), peer)))
            c_copies.append(send(piece, piece, c_sems, at_b(i, k, 0), sibling))
        pending.extend([copy for _, _, copy in b_copies])
        b_all[i], c_all[i] = b_copies, c_copies

    def share(i):
        if gathered:
            return
        for k, j, copy in b_all[i]:
            copy.wait_recv()
            piece = block(i, from_f(k), from_h(j))
            c_all[i].append(send(piece, piece, c_sems, at_b(i, k, j), sibling))
        pending.extend(c_all[i])

    def arrive(i):
        if gathered:
            return
        for copy in c_all[i]:
            copy.wait_recv()

    for g in range(GROUPS):
        for copy in w_copies[3 * g : 3 * g + 3]:
            copy.wait()
        if not gathered:
            a_all[g] = start_a(g)
    for copy in oh_copies:
        copy.wait()
    if not gathered:
        a_all[GROUPS] = start_a(GROUPS)
    q_copies = [
        send(mine, pack_ref.at[me], q_sems, off, dp_peers[off]) for off in range(n_dp - 1)
    ]
    pending.extend(q_copies)
    pack_ref[me] = mine[...]
    x_copy.wait()
    spread(0)
    spread(1)

    def norm_rows_in(rows):
        n, inv = stats(x_ref[rows, :].astype(F32))
        x_norm[rows, :] = n
        inv_x[rows, :] = inv
        normed[rows, :] = (n * gain).astype(BF16)

    row_loop(rows_all, norm_rows_in)
    share(0)
    spread(2)
    if not gathered:
        a_head = start_a(steps)
    fill_bias(len_ref, bias, passages)
    low, keeps = half_masks()

    def sides(rows):
        return jnp.concatenate([rows * keeps[0], rows * keeps[1]], axis=0)

    def spans(p, b):
        queries = pl.ds(pl.multiple_of(p * PLEN + b * QB, QB), QB)
        keys = pl.ds(pl.multiple_of(p * PLEN + b * WIN, WIN), KB)
        return queries, keys

    def project(g):
        for part in range(3):
            cols = slice((g * 3 + part) * GW, (g * 3 + part + 1) * GW)
            rows = dot_nn(normed[...], w_ref[:, cols])
            if part == 0:
                rows = rows * HD**-0.5
            qkv_ref[:, cols] = rows.astype(BF16)

    def attend(g):
        def pair(it, carry):
            p, w = it // (GW // 128), lax.rem(it, GW // 128)
            at = head_at(g, w)
            out_at = pl.multiple_of(g * GW + w * 128, 128)
            slot = (p * (HEADS // 2) + g * (GW // 128) + w) * SPANS
            for b in range(SPANS):
                qrows, krows = spans(p, b)
                scores = dot_nt(
                    qkv_ref[krows, pl.ds(at + GW, 128)], sides(qkv_ref[qrows, pl.ds(at, 128)])
                )
                both = []
                for side in range(2):
                    lanes = slice(side * QB, (side + 1) * QB)
                    probs = probs_of(scores[:, lanes] + bias[p * SPANS + b])
                    saved[slot + b, :, lanes] = probs
                    both.append(probs.astype(BF16))
                out = dot_tn(jnp.concatenate(both, axis=1), qkv_ref[krows, pl.ds(at + 2 * GW, 128)])
                ctx_ref[qrows, pl.ds(out_at, 128)] = jnp.where(low, out[:QB], out[QB:]).astype(BF16)
            return carry

        lax.fori_loop(0, passages * (GW // 128), pair, 0, unroll=UNROLL)

    arrive(0)
    project(0)
    attend(0)
    share(1)
    spread(GROUPS)
    arrive(1)
    project(1)
    attend(1)
    share(2)
    arrive(2)
    project(2)
    attend(2)
    share(GROUPS)
    for copy in q_copies:
        copy.wait_recv()

    def out_project(n):
        half = lax.rem(lax.rem(me, 2) + n, 2)
        cols = pl.ds(pl.multiple_of(half * (D // 2), 128), D // 2)
        res[:, cols] = x_ref[:, cols].astype(F32) + dot_nn(ctx_ref[...], outw_ref[:, cols])

    h_copies = []
    if not gathered:
        for k in range(1, n_f):
            a_head[k - 1].wait_recv()
            piece = head_half(from_f(k))
            h_copies.append(send(piece, piece, c_sems, at_b(GROUPS, n_f, k - 1), sibling))
    pending.extend(h_copies)
    out_project(0)
    arrive(GROUPS)
    out_project(1)
    for copy in h_copies:
        copy.wait_recv()

    def norm_rows(rows):
        n, inv = stats(res[rows, :])
        res[rows, :] = n
        inv_res[rows, :] = inv
        pooled[rows, :] = (n * fgain).astype(BF16)

    row_loop(rows_all, norm_rows)
    emb[...] = dot_nn(pooled[...], headw_ref[...])
    embedded = emb[...]
    inv_len = lax.rsqrt(jnp.sum(embedded * embedded, axis=-1, keepdims=True) + vec_eps)
    vectors = (embedded * inv_len).astype(BF16)
    q_near = passages * QLEN
    target = partner_ref[me]
    source = jnp.int32(0)
    for d in range(n_dp):
        source = jnp.where(partner_ref[d] == me, d, source)
    packs = (pack_ref[me], pack_ref[source])
    qf = jnp.concatenate([pack[:q_near].astype(F32) for pack in packs], axis=0)
    token = lax.broadcasted_iota(jnp.int32, (QLEN, CDIM), 0).astype(F32)
    masks = []
    for pack in packs:
        lens = pack[q_near : q_near + 16].astype(F32)
        for a in range(passages):
            masks.append(jnp.where(token < lens[a : a + 1], 1.0, 0.0))
    qmask = jnp.concatenate(masks, axis=0)[:, 0:1]
    qv = (qf * lax.rsqrt(jnp.sum(qf * qf, axis=-1, keepdims=True) + vec_eps)).astype(BF16)
    slot = lax.broadcasted_iota(jnp.int32, (1, PLEN), 1)
    live = jnp.concatenate(
        [jnp.where(slot < len_ref[b], 1.0, 0.0) for b in range(passages)], axis=1
    )
    weight = jnp.exp(dot_nt(qv, vectors) * (1.0 / soft_temp)) * live
    dens = [
        jnp.sum(weight[:, b * PLEN : (b + 1) * PLEN], axis=-1, keepdims=True)
        for b in range(passages)
    ]
    terms = [qmask * soft_temp * jnp.log(den) for den in dens]
    for q in range(2 * passages):
        for b in range(passages):
            total = jnp.sum(terms[b][q * QLEN : (q + 1) * QLEN], axis=0, keepdims=True)
            tile[q * passages + b : q * passages + b + 1, :] = jnp.broadcast_to(total, (1, 128))

    m_copies = [send(tile, got.at[me], m_sems, off, dp_peers[off]) for off in range(n_dp - 1)]
    got[me] = tile[...]

    def turn_context(n, cols):
        ctx_t[cols, :] = ctx_ref[:, cols].T

    block_loop(D, turn_context)
    for copy in m_copies:
        copy.wait()
    own = tile[...]
    from_target = got[target]
    from_source = got[source]
    half = passages * passages

    def logits_of(local, far, a):
        parts = [local[a * passages + b : a * passages + b + 1] for b in range(passages)]
        parts += [
            far[half + a * passages + b : half + a * passages + b + 1] for b in range(passages)
        ]
        total = jnp.exp(parts[0])
        for part in parts[1:]:
            total = total + jnp.exp(part)
        return parts, jnp.log(total)

    coef = [[] for _ in range(passages)]
    loss_ref[...] = jnp.zeros_like(loss_ref)
    for a in range(passages):
        parts, log_total = logits_of(own, from_target, a)
        loss_ref[a : a + 1, :] = log_total - parts[a]
        for b in range(passages):
            grad = jnp.exp(parts[b] - log_total) - (1.0 if a == b else 0.0)
            coef[b].append(jnp.broadcast_to(grad, (QLEN, 128)))
    for a in range(passages):
        parts, log_total = logits_of(from_source, own, a)
        for b in range(passages):
            grad = jnp.exp(parts[passages + b] - log_total)
            coef[b].append(jnp.broadcast_to(grad, (QLEN, 128)))
    for b in range(passages):
        rows = slice(b * PLEN, (b + 1) * PLEN)
        factor = jnp.concatenate(coef[b], axis=0)[:, 0:1] * qmask / dens[b]
        sim_grad = (weight[:, rows] * factor).astype(BF16)
        near = dot_tn(sim_grad[:q_near], qv[:q_near])
        far = dot_tn(sim_grad[q_near:], qv[q_near:]).astype(BF16).astype(F32)
        vgrad = near + far
        e, il = embedded[rows], inv_len[rows]
        along = jnp.sum(e * vgrad, axis=-1, keepdims=True)
        emb[rows, :] = il * vgrad - e * (il * il * il) * along
    emb_grad = emb[...].astype(BF16)
    wgrad_ref[:, D:] = dot_tn(pooled[...], emb_grad)

    def pool_back(n, cols):
        rg_ref[:, cols] = dot_nt(emb_grad, headw_ref[cols, :])

    block_loop(D, pool_back)

    def norm_back(rows):
        s = rg_ref[rows, :] * fgain
        n = res[rows, :]
        grad = inv_res[rows, :] * (
            s
            - jnp.mean(s, axis=-1, keepdims=True)
            - n * jnp.mean(s * n, axis=-1, keepdims=True)
        )
        rg_ref[rows, :] = grad
        rgb[rows, :] = grad.astype(BF16)

    row_loop(rows_all, norm_back)

    def out_back(n, cols):
        wgrad_ref[cols, :D] = dot_nn(ctx_t[cols, :], rgb[...])

    block_loop(D, out_back)

    thin = s3.shape[0]
    used = shard // thin
    quads = n_dp // 2
    my_h, my_c = me // 2, lax.rem(me, 2)
    pair = {"dp": 2 * my_h + 1 - my_c}
    near_quads = [lax.rem(my_h + off, quads) for off in range(1, quads)]
    near_rows = [lax.rem(my_f + off, n_f) for off in range(1, n_f)]

    def to_pair(stage, r0, sems, cols):
        for d in range(n_dp):
            for f in range(n_f):
                if d < used:
                    piece = wgrad_ref[f * shard + d * thin : f * shard + (d + 1) * thin, cols]
                    stage[d, f] = piece.astype(BF16)
                else:
                    stage[d, f] = jnp.zeros(stage.shape[2:], BF16)
        return [
            send(stage.at[2 * hh + 1 - my_c], r0.at[hh], sems, hh, pair) for hh in range(quads)
        ]

    def to_quads(src, dst, sems):
        return [
            send(src.at[hh], dst.at[my_h], sems, i, {"dp": 2 * hh + my_c})
            for i, hh in enumerate(near_quads)
        ]

    def to_rows(src, dst, sems):
        return [
            send(src.at[f], dst.at[my_f], sems, i, f_peers[i]) for i, f in enumerate(near_rows)
        ]

    def landed(copies):
        for copy in copies:
            copy.wait_recv()

    g0_a = to_pair(stage_a, r0_a, c0_sems, slice(0, FIRST))
    g0_b = to_pair(stage_b, r0_b, c1_sems, slice(FIRST, D + CDIM))

    def context_back(n, cols):
        dctx_ref[:, cols] = dot_nt(rgb[...], outw_ref[cols, :]).astype(BF16)

    block_loop(D, context_back)

    pairs = HEADS // 2

    def heads(first, last):
        def pair(it, carry):
            p, hp = it // pairs, lax.rem(it, pairs)
            at = head_at(hp // (GW // 128), lax.rem(hp, GW // 128))
            d_at = pl.multiple_of(hp * 128, 128)
            kg, vg = [], []
            for b in range(SPANS):
                qrows, krows = spans(p, b)
                q2 = sides(qkv_ref[qrows, pl.ds(at, 128)])
                d2 = sides(dctx_ref[qrows, pl.ds(d_at, 128)])
                k2 = qkv_ref[krows, pl.ds(at + GW, 128)]
                prob_grad = dot_nt(qkv_ref[krows, pl.ds(at + 2 * GW, 128)], d2)
                probs_b, score_b = [], []
                for side in range(2):
                    lanes = slice(side * QB, (side + 1) * QB)
                    probs, grad = saved[it * SPANS + b, :, lanes], prob_grad[:, lanes]
                    inner = jnp.sum(probs * grad, axis=0, keepdims=True)
                    probs_b.append(probs.astype(BF16))
                    score_b.append((probs * (grad - inner)).astype(BF16))
                score_grad = jnp.concatenate(score_b, axis=1)
                vg.append(dot_nn(jnp.concatenate(probs_b, axis=1), d2))
                kg.append(dot_nn(score_grad, q2))
                qg = dot_tn(score_grad, k2)
                qg = jnp.where(low, qg[:QB], qg[QB:]) * HD**-0.5
                grads[qrows, pl.ds(at, 128)] = qg.astype(BF16)
            rows = pl.ds(pl.multiple_of(p * PLEN, PLEN), PLEN)
            for offset, parts in ((GW, kg), (2 * GW, vg)):
                lower, upper = parts
                whole = jnp.concatenate(
                    [lower[:WIN], lower[WIN:] + upper[: KB - WIN], upper[KB - WIN :]], axis=0
                )
                grads[rows, pl.ds(at + offset, 128)] = whole.astype(BF16)
            return carry

        lax.fori_loop(first, last, pair, 0, unroll=UNROLL)

    heads(0, 2)
    landed(g0_a)
    for hh in range(quads):
        for f in range(n_f):
            both = stage_a[2 * hh + my_c, f].astype(F32) + r0_a[hh, f].astype(F32)
            pre_a[hh, f] = both.astype(BF16)
    g1_a = to_quads(pre_a, r1_a, h_sems)
    landed(g0_b)
    for f in range(n_f):
        for hh in range(quads):
            both = stage_b[2 * hh + my_c, f].astype(F32) + r0_b[hh, f].astype(F32)
            pre_b[f, hh] = both.astype(BF16)
    g1_b = to_rows(pre_b, r1_b, zb_sems)
    heads(2, passages * pairs)
    landed(g1_a)
    for f in range(n_f):
        total = pre_a[my_h, f].astype(F32)
        for hh in near_quads:
            total = total + r1_a[hh, f].astype(F32)
        acc_a[f] = total
        s2_a[f] = total.astype(BF16)
    g2_a = to_rows(s2_a, r2_a, z_sems)
    landed(g1_b)
    for hh in range(quads):
        total = pre_b[my_f, hh].astype(F32)
        for f in near_rows:
            total = total + r1_b[f, hh].astype(F32)
        acc_b[hh] = total
        s2_b[hh] = total.astype(BF16)
    g2_b = to_quads(s2_b, r2_b, hb_sems)

    def project_back(n, cols):
        res[:, cols] = dot_nt(grads[...], w_ref[cols, :])

    block_loop(D, project_back)
    landed(g2_a)
    total = acc_a[my_f]
    for f in near_rows:
        total = total + r2_a[f].astype(F32)
    s3[:, :FIRST] = total.astype(BF16)
    landed(g2_b)
    total = acc_b[my_h]
    for hh in near_quads:
        total = total + r2_b[hh].astype(F32)
    s3[:, FIRST:] = total.astype(BF16)
    g3 = [send(s3, r3.at[me], g3_sems, off, dp_peers[off]) for off in range(n_dp - 1)]
    r3[me] = s3[...]

    def norm_back_in(rows):
        n = x_norm[rows, :]
        t = res[rows, :] * gain
        grad = inv_x[rows, :] * (
            t
            - jnp.mean(t, axis=-1, keepdims=True)
            - n * jnp.mean(t * n, axis=-1, keepdims=True)
        )
        gin_ref[rows, :] = (rg_ref[rows, :] + grad).astype(BF16)

    row_loop(rows_all, norm_back_in)
    for copy in g3:
        copy.wait_recv()
    for d in range(used):
        piece = r3[d].astype(F32)
        gout_ref[d * thin : (d + 1) * thin, :] = piece[:, :D]
        ghead_ref[d * thin : (d + 1) * thin, :] = piece[:, D:]
    for copy in pending + g0_a + g0_b + g1_a + g1_b + g2_a + g2_b + g3:
        copy.wait_send()


def finish_kernel(gin, gout, ghead, loss, gin_out, gout_out, ghead_out, loss_out, sems):
    copies = [
        pltpu.make_async_copy(source, target, sems.at[i])
        for i, (source, target) in enumerate(
            ((gin, gin_out), (gout, gout_out), (ghead, ghead_out))
        )
    ]
    for copy in copies:
        copy.start()
    for a in range(loss_out.shape[0]):
        loss_out[a] = jnp.max(loss[a : a + 1, :])
    for copy in copies:
        copy.wait()


VM = pl.BlockSpec(memory_space=pltpu.VMEM)
SM = pl.BlockSpec(memory_space=pltpu.SMEM)
HB = pl.BlockSpec(memory_space=pl.ANY)
VMEM_LIMIT = 56 << 20


def sem_pair(count):
    return [pltpu.SemaphoreType.DMA((count,))] * 2


def per_device(
    n_dp,
    n_f,
    hidden_in,
    norm_gain,
    qkv_weight,
    out_weight,
    final_gain,
    head_weight,
    queries,
    query_lengths,
    passage_lengths,
    partner,
):
    tok = hidden_in.shape[0]
    count = passage_lengths.shape[0]
    qrows = count * QLEN
    shape = jax.ShapeDtypeStruct
    shard = qkv_weight.shape[0]
    weights = (qkv_weight, out_weight, head_weight)
    gathered = n_dp % 2 != 0 or shard % (8 * n_dp) != 0
    if gathered:
        weights = tuple(lax.all_gather(w, "fsdp", axis=0, tiled=True) for w in weights)
    copies = (n_f - 1) * n_dp // 2
    steps = GROUPS + 1
    extra = (
        []
        if gathered
        else sem_pair((steps + 1) * (n_f - 1))
        + sem_pair(steps * copies)
        + sem_pair(steps * copies + n_f - 1)
    )
    thin = -(-shard // (8 * n_dp)) * 8
    wide = D + CDIM
    held = pl.pallas_call(
        functools.partial(step_kernel, n_dp, n_f, gathered),
        out_shape=(
            pltpu.VMEM((tok, D), BF16),
            pltpu.VMEM((shard, D), F32),
            pltpu.VMEM((shard, CDIM), F32),
            pltpu.VMEM((8, 128), F32),
        ),
        in_specs=[HB, SM, SM, SM, VM, VM, VM, HB, HB, HB],
        out_specs=(VM,) * 4,
        scratch_shapes=[
            pltpu.VMEM((tok, D), BF16),
            pltpu.VMEM((D, 3 * D), BF16),
            pltpu.VMEM((D, D), BF16),
            pltpu.VMEM((D, CDIM), BF16),
            pltpu.VMEM((tok, 3 * D), BF16),
            pltpu.VMEM((tok, D), BF16),
            pltpu.VMEM((D, tok), BF16),
            pltpu.VMEM((n_dp, qrows + 16, CDIM), BF16),
            pltpu.VMEM((tok, D), BF16),
            pltpu.VMEM((tok, D), F32),
            pltpu.VMEM((tok, 1), F32),
            pltpu.VMEM((qrows + 16, CDIM), BF16),
            pltpu.VMEM((tok, D), F32),
            pltpu.VMEM((tok, 1), F32),
            pltpu.VMEM((tok, D), BF16),
            pltpu.VMEM((tok, CDIM), F32),
            pltpu.VMEM((tok, D), BF16),
            pltpu.VMEM((tok, D), F32),
            pltpu.VMEM((tok, D), BF16),
            pltpu.VMEM((D, wide), F32),
            pltpu.VMEM((tok, 3 * D), BF16),
            pltpu.VMEM((count * SPANS, KB, QB), F32),
            pltpu.VMEM((count * (HEADS // 2) * SPANS, KB, 2 * QB), F32),
            pltpu.VMEM((2 * count * count, 128), F32),
            pltpu.VMEM((n_dp, 2 * count * count, 128), F32),
            pltpu.VMEM((n_dp, n_f, thin, FIRST), BF16),
            pltpu.VMEM((n_dp // 2, n_f, thin, FIRST), BF16),
            pltpu.VMEM((n_dp // 2, n_f, thin, FIRST), BF16),
            pltpu.VMEM((n_dp // 2, n_f, thin, FIRST), BF16),
            pltpu.VMEM((n_f, thin, FIRST), F32),
            pltpu.VMEM((n_f, thin, FIRST), BF16),
            pltpu.VMEM((n_f, thin, FIRST), BF16),
            pltpu.VMEM((n_dp, n_f, thin, wide - FIRST), BF16),
            pltpu.VMEM((n_dp // 2, n_f, thin, wide - FIRST), BF16),
            pltpu.VMEM((n_f, n_dp // 2, thin, wide - FIRST), BF16),
            pltpu.VMEM((n_f, n_dp // 2, thin, wide - FIRST), BF16),
            pltpu.VMEM((n_dp // 2, thin, wide - FIRST), F32),
            pltpu.VMEM((n_dp // 2, thin, wide - FIRST), BF16),
            pltpu.VMEM((n_dp // 2, thin, wide - FIRST), BF16),
            pltpu.VMEM((thin, wide), BF16),
            pltpu.VMEM((n_dp, thin, wide), BF16),
        ]
        + sem_pair(n_dp - 1)
        + sem_pair(n_dp - 1)
        + sem_pair(n_dp // 2)
        + sem_pair(n_dp // 2)
        + sem_pair(n_dp // 2 - 1)
        + sem_pair(n_f - 1)
        + sem_pair(n_f - 1)
        + sem_pair(n_dp // 2 - 1)
        + sem_pair(n_dp - 1)
        + [pltpu.SemaphoreType.DMA((3 + 3 * GROUPS,))]
        + extra,
        compiler_params=pltpu.CompilerParams(
            vmem_limit_bytes=VMEM_LIMIT, collective_id=1, has_side_effects=True
        ),
        name="step",
    )(
        hidden_in,
        passage_lengths,
        query_lengths,
        partner,
        norm_gain,
        final_gain,
        queries.reshape(qrows, CDIM),
        *weights,
    )
    grad_input, grad_out, grad_head, losses = pl.pallas_call(
        finish_kernel,
        out_shape=(
            shape((tok, D), BF16),
            shape((shard, D), F32),
            shape((shard, CDIM), F32),
            shape((count,), F32),
        ),
        in_specs=[VM] * 4,
        out_specs=(HB, HB, HB, SM),
        scratch_shapes=[pltpu.SemaphoreType.DMA((3,))],
        compiler_params=pltpu.CompilerParams(vmem_limit_bytes=4 << 20),
        name="finish",
    )(*[pltpu.with_memory_space_constraint(a, pltpu.VMEM) for a in held])
    return losses, grad_input, grad_out, grad_head


def solution(mesh):
    placed = (
        P(("dp", "fsdp"), None),
        P(),
        P("fsdp", None),
        P("fsdp", None),
        P(),
        P("fsdp", None),
        P(("dp", "fsdp"), None, None),
        P(("dp", "fsdp")),
        P(("dp", "fsdp")),
        P(),
    )
    return jax.shard_map(
        functools.partial(per_device, mesh.shape["dp"], mesh.shape["fsdp"]),
        mesh=mesh,
        in_specs=placed,
        out_specs=(P(("dp", "fsdp")), P(("dp", "fsdp"), None), P("fsdp", None), P("fsdp", None)),
        check_vma=False,
    )
```
